32 devices in a mesh: dp: 32 (over z, y, x, core).
Axes of the slice: x: 2, y: 2, z: 4, core: 2. Of those that a mesh axis runs over, the one named last changes fastest.
Arguments:
- block_in: bfloat16 [12608, 768], P('dp'), may hold values from -6 to 6
- slot_mask: int32 [12608], P('dp'), may hold values from 0 to 1, as said below
- gain_first: bfloat16 [768], P('dp'), may hold values from 0.5 to 1.5
- shift_first: bfloat16 [768], P('dp'), may hold values from -3 to 3
- packed_weight: bfloat16 [768, 2304], P('dp'), may hold values from -0.21875 to 0.21875
- query_bias: bfloat16 [768], P('dp'), may hold values from -3 to 3
- value_bias: bfloat16 [768], P('dp'), may hold values from -3 to 3
- out_weight: bfloat16 [768, 768], P('dp'), may hold values from -1.75 to 1.75
- out_bias: bfloat16 [768], P('dp'), may hold values from -3 to 3
- gain_second: bfloat16 [768], P('dp'), may hold values from 0.5 to 1.5
- shift_second: bfloat16 [768], P('dp'), may hold values from -3 to 3
- up_weight: bfloat16 [768, 3072], P('dp'), may hold values from -0.21875 to 0.21875
- up_bias: bfloat16 [3072], P('dp'), may hold values from -3 to 3
- down_weight: bfloat16 [3072, 768], P('dp'), may hold values from -0.109375 to 0.109375
- down_bias: bfloat16 [768], P('dp'), may hold values from -3 to 3
- cotangent: bfloat16 [12608, 768], P('dp'), may hold values from -6 to 6
Outputs:
- block_out: bfloat16 [12608, 768], P('dp')
- input_grad: float32 [12608, 768], P('dp')
- grad_gain_first: float32 [768], P('dp')
- grad_shift_first: float32 [768], P('dp')
- grad_packed_weight: float32 [768, 2304], P('dp')
- grad_query_bias: float32 [768], P('dp')
- grad_value_bias: float32 [768], P('dp')
- grad_out_weight: float32 [768, 768], P('dp')
- grad_out_bias: float32 [768], P('dp')
- grad_gain_second: float32 [768], P('dp')
- grad_shift_second: float32 [768], P('dp')
- grad_up_weight: float32 [768, 3072], P('dp')
- grad_up_bias: float32 [3072], P('dp')
- grad_down_weight: float32 [3072, 768], P('dp')
- grad_down_bias: float32 [768], P('dp')
The draws below stay inside these ranges and needn't reach their ends.
Inputs may be any that keep to these rules, and one draw needn't show every extreme that they name: `slot_mask`: each image slot of 197 tokens is all ones or all zeros; on each device the live image slots come first; each device has at least 1 of its 2 image slots live, and some device has both live.
All inputs are finite; a program needn't handle non-finite values.
Results may differ from the reference program's by a relative error of at most 0.011.
Values may be sent and summed in bfloat16 or wider, within the bound.
No kernel may reach another device: no remote copies, remote signals or barrier semaphores. Data moves between devices by JAX's collectives and lax.ppermute only.
A program may use at most 192 MiB of HBM per device.

```python
import jax
import jax.numpy as jnp
from jax import lax

D = 768
HEADS = 12
HEAD_DIM = 64
FF = 3072
LEN = 197
IMG_MAX = 2
TOKENS = 12608
IMAGES = 64


def draw_slot_mask(key, part):
    devices = IMAGES // IMG_MAX
    counts = jax.random.randint(jax.random.fold_in(key, 11), (devices,), IMG_MAX // 2, IMG_MAX + 1)
    fullest = jax.random.randint(jax.random.fold_in(key, 12), (), 0, devices)
    counts = jnp.where(jnp.arange(devices) == fullest, IMG_MAX, counts)
    slot_index = jnp.arange(devices * IMG_MAX * LEN)
    owner = slot_index // (IMG_MAX * LEN)
    image_slot = slot_index % (IMG_MAX * LEN) // LEN
    return (image_slot < counts[owner]).astype(jnp.int32)


def strengthened(values, rng, source, target, parts, factor):
    owner, partner = [(jnp.arange(values.shape[position]) // (values.shape[position] // parts)).reshape([-1 if axis == position else 1 for axis in range(values.ndim)]) for position in (source, target)]
    chosen = jax.random.permutation(rng, parts)[partner]
    strong = (owner == chosen) | (owner == (partner + parts // 2) % parts)
    return jnp.where(strong, factor * values, values)


def block_levels(key, extent, shards, smallest, top_value):
    def one(dim, parts):
        steps = jax.random.uniform(jax.random.fold_in(jax.random.fold_in(key, 6), dim), (parts,), jnp.float32, smallest / len(shards), top_value / len(shards))
        return jnp.repeat(jnp.exp(steps), extent[dim] // parts).reshape((-1,) + (1,) * (len(extent) - dim - 1))

    loudness = one(*shards[0])
    for cut in shards[1:]:
        loudness = loudness * one(*cut)
    return loudness


def normal_values(rng, extent, spread, most, split=(), held_as=jnp.bfloat16):
    result = spread * jax.random.normal(rng, extent, jnp.float32)
    if split:
        result = result * block_levels(rng, extent, split, -0.22, 0.18)
    return jnp.clip(result, -most, most).astype(held_as)


def gaussian_with(own_key, extent, spread, reach, cuts, heavy, kind=jnp.bfloat16):
    drawn = spread * jax.random.normal(own_key, extent, jnp.float32)
    if cuts:
        drawn = drawn * block_levels(own_key, extent, cuts, -0.22, 0.18)
    return jnp.clip(strengthened(drawn, jax.random.fold_in(own_key, 3), *heavy), -reach, reach).astype(kind)


def setup_inputs(seed: int = 0) -> dict:
    seeds = jax.random.split(jax.random.key(seed), 17)
    block_in = gaussian_with(seeds[0], (TOKENS, D), 1.0, 6.0, ((0, 32),), (0, 1, 32, 2.75))
    slot_mask = draw_slot_mask(jax.random.fold_in(seeds[16], 71), 0)
    gain_first = jnp.clip(1.0 + 0.1 * jax.random.normal(seeds[2], (D,), jnp.float32), 0.5, 1.5).astype(jnp.bfloat16)
    shift_first = normal_values(seeds[3], (D,), 0.5, 3.0, ((0, 32),))
    packed_weight = normal_values(seeds[4], (D, 3 * D), D ** -0.5, 0.21875, ((0, 32),))
    query_bias = normal_values(seeds[5], (D,), 0.5, 3.0, ((0, 32),))
    value_bias = normal_values(seeds[6], (D,), 0.5, 3.0, ((0, 32),))
    out_weight = normal_values(seeds[7], (D, D), (D // 64) ** -0.5, 1.75, ((0, 32),))
    out_bias = normal_values(seeds[8], (D,), 0.5, 3.0, ((0, 32),))
    gain_second = jnp.clip(1.0 + 0.1 * jax.random.normal(seeds[9], (D,), jnp.float32), 0.5, 1.5).astype(jnp.bfloat16)
    shift_second = normal_values(seeds[10], (D,), 0.5, 3.0, ((0, 32),))
    up_weight = normal_values(seeds[11], (D, FF), D ** -0.5, 0.21875, ((0, 32),))
    up_bias = normal_values(seeds[12], (FF,), 0.5, 3.0, ((0, 32),))
    down_weight = normal_values(seeds[13], (FF, D), FF ** -0.5, 0.109375, ((0, 32),))
    down_bias = normal_values(seeds[14], (D,), 0.5, 3.0, ((0, 32),))
    cotangent = gaussian_with(seeds[15], (TOKENS, D), 1.0, 6.0, ((0, 32),), (0, 1, 32, 2.75))
    return dict(block_in=block_in, slot_mask=slot_mask, gain_first=gain_first, shift_first=shift_first, packed_weight=packed_weight, query_bias=query_bias, value_bias=value_bias, out_weight=out_weight, out_bias=out_bias, gain_second=gain_second, shift_second=shift_second, up_weight=up_weight, up_bias=up_bias, down_weight=down_weight, down_bias=down_bias, cotangent=cotangent)


@jax.custom_vjp
def low(v):
    return lax.optimization_barrier(v.astype(jnp.bfloat16)).astype(jnp.float32)

@jax.custom_vjp
def low_back(v):
    return v

def low_keep(v):
    return (low(v), None)

def low_pass(kept, grad):
    return (grad,)

def back_keep(v):
    return (v, None)

def back_low(kept, grad):
    return (low(grad),)
low.defvjp(low_keep, low_pass)
low_back.defvjp(back_keep, back_low)

def layer_norm(values, gain, shift):
    centre_mean = lax.optimization_barrier(jnp.mean(values, axis=-1, keepdims=True))
    centred = values - centre_mean
    variance = lax.optimization_barrier(jnp.mean(centred * centred, axis=-1, keepdims=True))
    return centred * lax.rsqrt(variance + 1e-06) * gain + shift

def forward(params, inputs, live_mask):
    gain_first, shift_first, packed_weight, query_bias, value_bias, out_weight, out_bias, gain_second, shift_second, up_weight, up_bias, down_weight, down_bias = params
    highest = lax.Precision.HIGHEST
    batch, length, width = inputs.shape
    normed = low(layer_norm(inputs, gain_first, shift_first))
    packed = jnp.einsum('gtd,de->gte', normed, packed_weight, precision=highest)
    packed = packed.reshape(batch, length, 3, HEADS, HEAD_DIM)
    query = low(low_back(packed[:, :, 0] + query_bias.reshape(HEADS, HEAD_DIM)))
    key_low = low(low_back(packed[:, :, 1]))
    value_low = low(low_back(packed[:, :, 2] + value_bias.reshape(HEADS, HEAD_DIM)))
    scores = low_back(jnp.einsum('gqhe,gkhe->ghqk', query, key_low, precision=highest) * HEAD_DIM ** (-0.5))
    attn_weights = low(jax.nn.softmax(scores, axis=-1))
    mixed = jnp.einsum('ghqk,gkhe->gqhe', attn_weights, value_low, precision=highest)
    attended = low(low_back(mixed)).reshape(batch, length, width)
    branch = low_back(jnp.einsum('gtd,de->gte', attended, out_weight, precision=highest) + out_bias)
    middle = inputs + branch
    normed_two = low(layer_norm(middle, gain_second, shift_second))
    pre_act = low_back(jnp.einsum('gtd,df->gtf', normed_two, up_weight, precision=highest) + up_bias)
    activated = low(jax.nn.gelu(pre_act, approximate=False))
    mlp_out = low_back(jnp.einsum('gtf,fd->gtd', activated, down_weight, precision=highest) + down_bias)
    return (middle + mlp_out) * live_mask[:, :, None]

def reference(block_in, slot_mask, gain_first, shift_first, packed_weight, query_bias, value_bias, out_weight, out_bias, gain_second, shift_second, up_weight, up_bias, down_weight, down_bias, cotangent):
    params = tuple((piece.astype(jnp.float32) for piece in (gain_first, shift_first, packed_weight, query_bias, value_bias, out_weight, out_bias, gain_second, shift_second, up_weight, up_bias, down_weight, down_bias)))
    groups = IMAGES // 16
    inputs = block_in.astype(jnp.float32).reshape(groups, 16, LEN, D)
    masks = slot_mask.astype(jnp.float32).reshape(groups, 16, LEN)
    cotans = cotangent.astype(jnp.float32).reshape(groups, 16, LEN, D)

    def step(carry, item):
        group_in, group_mask, group_cot = item
        outputs, pull = jax.vjp(lambda par, val: forward(par, val, group_mask), params, group_in)
        grad_params, grad_input = pull(group_cot)
        summed = tuple((total + piece for total, piece in zip(carry, grad_params)))
        return (summed, (outputs.astype(jnp.bfloat16), grad_input))
    zeros = tuple((jnp.zeros(piece.shape, jnp.float32) for piece in params))
    totals, (outputs, grads) = lax.scan(step, zeros, (inputs, masks, cotans))
    return (outputs.reshape(IMAGES * LEN, D), grads.reshape(IMAGES * LEN, D), totals[0], totals[1], totals[2], totals[3], totals[4], totals[5], totals[6], totals[7], totals[8], totals[9], totals[10], totals[11], totals[12])
```

```python
import jax
import jax.numpy as jnp
from jax import lax
from jax.sharding import PartitionSpec as P

D = 768
HEADS = 12
HEAD_DIM = 64
LEN = 197
F32 = jnp.float32
BF16 = jnp.bfloat16


def layer_norm(values, gain, shift):
    centre_mean = jnp.mean(values, axis=-1, keepdims=True)
    centred = values - centre_mean
    variance = jnp.mean(centred * centred, axis=-1, keepdims=True)
    return centred * lax.rsqrt(variance + 1e-06) * gain + shift


def row_sum(values):
    return jnp.sum(values, axis=0, dtype=F32)


class Links:
    def __init__(self, count):
        chips = count // 2
        z = min(4, chips)
        plane = chips // z
        x = 1
        while x * x < plane:
            x *= 2
        self.count = count
        self.index = lax.axis_index("dp")
        bit = 2
        self.x_bits, self.y_bits, self.z_bits = [], [], []
        for bits, extent in ((self.x_bits, x), (self.y_bits, plane // x), (self.z_bits, z)):
            size = 1
            while size < extent:
                bits.append(bit)
                bit *= 2
                size *= 2
        self.core = self.index % 2

    def swap(self, value, even, odd):
        pairs = [(i, i ^ (odd if i % 2 else even)) for i in range(self.count)]
        return lax.ppermute(value, "dp", pairs)

    def side(self, even, odd):
        mask = jnp.where(self.core == 0, even, odd)
        return (self.index & mask) != 0

    def gather(self, shard):
        rows, cols = shard.shape
        held = shard[None]
        steps = [(bit, bit) for bit in reversed(self.z_bits)]
        steps += list(zip(self.x_bits + self.y_bits, self.y_bits + self.x_bits))
        for even, odd in steps:
            other = self.swap(held, even, odd)
            high = self.side(even, odd)
            first = jnp.where(high, other, held)
            second = jnp.where(high, held, other)
            held = jnp.concatenate([first[None], second[None]])
            held = held.reshape((-1, rows, cols))
        other = self.swap(held, 1, 1)
        even = jnp.where(self.core == 0, held, other)
        odd = jnp.where(self.core == 0, other, held)
        flips = len(steps)
        shape = (2,) * flips
        even_bits = [s[0] for s in reversed(steps)]
        odd_bits = [s[1] for s in reversed(steps)]
        order = sorted(range(flips), key=lambda i: -even_bits[i])
        even = even.reshape(shape + (rows, cols)).transpose(order + [flips, flips + 1])
        order = sorted(range(flips), key=lambda i: -odd_bits[i])
        odd = odd.reshape(shape + (rows, cols)).transpose(order + [flips, flips + 1])
        full = jnp.stack([even, odd], axis=flips)
        return full.reshape(self.count * rows, cols)

    def scatter(self, partial):
        rows, cols = partial.shape[0] // self.count, partial.shape[1]
        steps = [(bit, bit) for bit in reversed(self.z_bits)]
        steps += list(zip(self.x_bits + self.y_bits, self.y_bits + self.x_bits))
        steps = steps[::-1]
        flips = len(steps)
        blocks = partial.astype(BF16).reshape((2,) * flips + (2, rows, cols))
        all_bits = sorted((s[0] for s in steps), reverse=True)
        tail = [flips, flips + 1]
        even = blocks[(slice(None),) * flips + (0,)].transpose([all_bits.index(s[0]) for s in steps] + tail)
        odd = blocks[(slice(None),) * flips + (1,)].transpose([all_bits.index(s[1]) for s in steps] + tail)
        even = even.reshape(-1, rows, cols)
        odd = odd.reshape(-1, rows, cols)
        mine = self.core == 0
        other = self.swap(jnp.where(mine, odd, even), 1, 1)
        total = jnp.where(mine, even, odd).astype(F32) + other.astype(F32)
        for step in steps:
            half = total.shape[0] // 2
            high = self.side(*step)
            low = total.astype(BF16)
            sent = jnp.where(high, low[:half], low[half:])
            other = self.swap(sent, *step)
            total = jnp.where(high, total[half:], total[:half]) + other.astype(F32)
        return total[0]


def shards(
    block_in,
    slot_mask,
    gain_first,
    shift_first,
    packed_weight,
    query_bias,
    value_bias,
    out_weight,
    out_bias,
    gain_second,
    shift_second,
    up_weight,
    up_bias,
    down_weight,
    down_bias,
    cotangent,
):
    links = Links(lax.axis_size("dp"))
    scale = HEAD_DIM ** (-0.5)
    own = packed_weight.shape[0]
    wide = up_bias.shape[0] // own
    columns = [gain_first, shift_first, query_bias, value_bias, out_bias, gain_second, shift_second, down_bias]
    columns = jnp.concatenate([jnp.stack(columns, axis=1), up_bias.reshape(own, wide)], axis=1)
    width = columns.shape[1]
    columns = jnp.pad(columns, ((0, 0), (0, 128 - width)))
    first = links.gather(jnp.concatenate([packed_weight, out_weight, columns], axis=1))
    full_packed = first[:, : 3 * D]
    full_out = first[:, 3 * D : 4 * D]
    vectors = first[:, 4 * D : 4 * D + width].astype(F32).T
    g1, c1, qbias, vbias, obias, g2, c2, dbias = (vectors[i] for i in range(8))
    ubias = vectors[8:].T.reshape(-1)
    full_up = links.gather(up_weight)
    full_down = links.gather(down_weight)

    tokens = block_in.shape[0]
    images = tokens // LEN
    inputs = block_in.astype(F32)
    live = slot_mask.astype(F32)[:, None]
    d_res = cotangent.astype(F32) * live
    d_mlp = d_res.astype(BF16)

    def heads_of(values):
        return values.reshape(images, LEN, HEADS, HEAD_DIM).transpose(0, 2, 1, 3)

    def tokens_of(values):
        return values.transpose(0, 2, 1, 3).reshape(tokens, D)

    def mul(a, b):
        return jnp.dot(a, b, preferred_element_type=F32)

    def mul_t(a, b):
        return lax.dot_general(a, b, (((1,), (1,)), ((), ())), preferred_element_type=F32)

    def t_mul(a, b):
        return lax.dot_general(a, b, (((0,), (0,)), ((), ())), preferred_element_type=F32)

    def each(spec, a, b):
        return jnp.einsum(spec, a, b, preferred_element_type=F32)

    normed_low = layer_norm(inputs, g1, c1).astype(BF16)
    packed = mul(normed_low, full_packed)
    query = heads_of((packed[:, :D] + qbias).astype(BF16))
    key_low = heads_of(packed[:, D : 2 * D].astype(BF16))
    value_low = heads_of((packed[:, 2 * D :] + vbias).astype(BF16))
    scores = each("ghqe,ghke->ghqk", query, key_low) * scale
    top_score = jnp.max(scores, axis=-1, keepdims=True)
    log_total = top_score + jnp.log(jnp.sum(jnp.exp(scores - top_score), axis=-1, keepdims=True))
    attn = jnp.exp(scores - log_total)
    attn_low = attn.astype(BF16)
    attended = tokens_of(each("ghqk,ghke->ghqe", attn_low, value_low).astype(BF16))
    middle = inputs + mul(attended, full_out) + obias
    normed_two = layer_norm(middle, g2, c2).astype(BF16)
    pre_act = mul(normed_two, full_up) + ubias
    activated_f, gelu_pull = jax.vjp(lambda v: jax.nn.gelu(v, approximate=False), pre_act)
    activated = activated_f.astype(BF16)
    grad_down_weight = links.scatter(t_mul(activated, d_mlp))
    block_out = ((middle + mul(activated, full_down) + dbias) * live).astype(BF16)

    d_act = mul_t(d_mlp, full_down)
    d_pre = gelu_pull(d_act)[0].astype(BF16)
    grad_up_weight = links.scatter(t_mul(normed_two, d_pre))
    d_normed_two = mul_t(d_pre, full_up)
    zero_shift = jnp.zeros((D,), F32)
    d_mid_part, grad_g2, grad_c2 = jax.vjp(layer_norm, middle, g2, zero_shift)[1](d_normed_two)
    d_middle = d_res + d_mid_part
    d_branch = d_middle.astype(BF16)
    grad_out = t_mul(attended, d_branch)
    d_att = heads_of(mul_t(d_branch, full_out).astype(BF16))
    d_values = each("ghqk,ghqe->ghke", attn_low, d_att).astype(BF16)
    d_attn = each("ghqe,ghke->ghqk", d_att, value_low)
    d_scores = (attn * (d_attn - jnp.sum(attn * d_attn, axis=-1, keepdims=True))).astype(BF16)
    d_query = (each("ghqk,ghke->ghqe", d_scores, key_low) * scale).astype(BF16)
    d_keys = (each("ghqk,ghqe->ghke", d_scores, query) * scale).astype(BF16)
    d_packed = jnp.concatenate([tokens_of(d_query), tokens_of(d_keys), tokens_of(d_values)], axis=1)
    grad_packed = t_mul(normed_low, d_packed)
    d_normed = mul_t(d_packed, full_packed)
    d_in_part, grad_g1, grad_c1 = jax.vjp(layer_norm, inputs, g1, zero_shift)[1](d_normed)
    input_grad = d_middle + d_in_part
    packed_sums = row_sum(d_packed)
    rows = [
        grad_g1,
        grad_c1,
        packed_sums[:D],
        packed_sums[2 * D :],
        row_sum(d_branch),
        grad_g2,
        grad_c2,
        row_sum(d_mlp),
    ]
    rows = jnp.stack(rows, axis=1)
    rows = jnp.concatenate([rows, row_sum(d_pre).reshape(D, wide)], axis=1)
    rows = jnp.pad(rows, ((0, 0), (0, 128 - width)))
    last = links.scatter(jnp.concatenate([grad_packed, grad_out, rows], axis=1))
    small = last[:, 4 * D :]
    return (
        block_out,
        input_grad,
        small[:, 0],
        small[:, 1],
        last[:, : 3 * D],
        small[:, 2],
        small[:, 3],
        last[:, 3 * D : 4 * D],
        small[:, 4],
        small[:, 5],
        small[:, 6],
        grad_up_weight,
        small[:, 8:width].reshape(-1),
        grad_down_weight,
        small[:, 7],
    )


def solution(mesh):
    row, flat = P("dp", None), P("dp")
    in_specs = (row, flat, flat, flat, row, flat, flat, row, flat, flat, flat, row, flat, row, flat, row)
    out_specs = (row, row, flat, flat, row, flat, flat, row, flat, flat, flat, row, flat, row, flat)
    return jax.shard_map(shards, mesh=mesh, in_specs=in_specs, out_specs=out_specs, check_vma=False)
```

```python
import functools

import jax
import jax.numpy as jnp
from jax import lax
from jax.experimental import pallas as pl
from jax.experimental.pallas import tpu as pltpu
from jax.sharding import PartitionSpec as P

D = 768
HEADS = 12
HEAD_DIM = 64
FF = 3072
LEN = 197
SLOT = 208
SPEED = 1.15e9
LENGTHS = (32, 0.25, 8, 24, 0.5, 0.25, 3, 0.25, 0.25, 8, 2, 4, 12, 8, 2, 0.25, 0.5, 24, 16, 1, 6, 1, 16, 24, 16, 0.25, 0.5, 16, 6, 2, 32, 0.5, 3, 8, 2)
SCALE = HEAD_DIM ** (-0.5)
F32 = jnp.float32
BF16 = jnp.bfloat16
VMEM = pl.BlockSpec(memory_space=pltpu.VMEM)
SMEM = pl.BlockSpec(memory_space=pltpu.SMEM)
ANY = pl.BlockSpec(memory_space=pl.ANY)


def params(megabytes):
    return pltpu.CompilerParams(
        vmem_limit_bytes=megabytes << 20, dimension_semantics=("arbitrary",)
    )


def cost(length):
    return pl.CostEstimate(flops=int(length * SPEED), transcendentals=0, bytes_accessed=D)


def mul(a, b):
    return jnp.dot(a, b, preferred_element_type=F32)


def mul_t(a, b):
    return lax.dot_general(a, b, (((1,), (1,)), ((), ())), preferred_element_type=F32)


def t_mul(a, b):
    return lax.dot_general(a, b, (((0,), (0,)), ((), ())), preferred_element_type=F32)


class Links:
    def __init__(self, count):
        chips = count // 2
        z = min(4, chips)
        plane = chips // z
        x = 1
        while x * x < plane:
            x *= 2
        self.count, self.z, self.plane = count, z, plane
        bit = 2
        x_bits, y_bits, z_bits = [], [], []
        for bits, extent in ((x_bits, x), (y_bits, plane // x), (z_bits, z)):
            size = 1
            while size < extent:
                bits.append(bit)
                bit *= 2
                size *= 2
        self.steps = [(b, b) for b in reversed(z_bits)]
        self.steps += list(zip(x_bits + y_bits, y_bits + x_bits))
        index = lax.axis_index("dp")
        core = index % 2
        sides = [((index & jnp.where(core == 0, *step)) != 0).astype(jnp.int32) for step in self.steps]
        self.place = jnp.stack([core.astype(jnp.int32)] + sides)
        self.last = None
        self.lengths = iter(LENGTHS + (1,) * 64)

    def length(self):
        return next(self.lengths)

    def run(self, kernel, *args, **options):
        out = kernel(self.last, *args, **options)
        self.last = out[0] if isinstance(out, (tuple, list)) else out
        return out

    def slot(self, device):
        place = 0
        for weight, step in enumerate(self.steps):
            if device & step[device % 2]:
                place |= 1 << weight
        return place // self.z, place % self.z

    def swap(self, value, even, odd):
        pairs = [(i, i ^ (odd if i % 2 else even)) for i in range(self.count)]
        return lax.ppermute(value, "dp", pairs)

    def pair(self, at, *parts):
        count, rows = parts[0][0].shape[:2]
        widths = [part[0].shape[2] for part in parts]
        flat = [part[0] for part in parts] + [part[1] for part in parts]

        def body(place, *refs):
            out = refs[-1]
            high = place[1 + at]

            def copy(i, carry):
                start = 0
                for k, width in enumerate(widths):
                    cols = pl.ds(start, width)
                    out[high, i, :, cols] = refs[k][i]
                    out[1 - high, i, :, cols] = refs[len(widths) + k][i]
                    start += width
                return carry

            lax.fori_loop(0, count, copy, 0)

        def kernel(last):
            joined = pl.pallas_call(
                body,
                out_shape=jax.ShapeDtypeStruct((2, count, rows, sum(widths)), BF16),
                in_specs=[SMEM] + [VMEM] * len(flat) + ([] if last is None else [ANY]),
                out_specs=VMEM,
                compiler_params=pltpu.CompilerParams(vmem_limit_bytes=24 << 20),
                cost_estimate=cost(self.length()),
                name="pair",
            )(self.place, *flat, *([] if last is None else [last]))
            return joined

        return self.run(kernel).reshape(2 * count, rows, sum(widths))

    def advance(self, held, first, last):
        for at in range(first, last):
            held = self.pair(at, (held, self.swap(held, *self.steps[at])))
        return held

    def across(self, held):
        held = held.reshape((self.plane, self.z) + held.shape[1:])
        return held, self.swap(held, 1, 1)

    def exchange(self, kept, sent):
        other = self.swap(sent, 1, 1)
        return kept.reshape((-1,) + kept.shape[2:]), other.reshape((-1,) + kept.shape[2:])

    def halve(self, at, kept, other):
        half = kept.shape[0] // 2
        chunk = max(1, half // 4)
        grid = half // chunk
        block = (chunk,) + kept.shape[1:]
        upper = pl.BlockSpec(block, lambda i, place: (place[1 + at] * grid + i, 0, 0))
        lower = pl.BlockSpec(block, lambda i, place: ((1 - place[1 + at]) * grid + i, 0, 0))
        straight = pl.BlockSpec(block, lambda i, place: (i, 0, 0))

        def body(place, kept_up, kept_low, other_up, other_low, last, stay, leave):
            stay[...] = kept_up[...].astype(F32) + other_up[...].astype(F32)
            leave[...] = (kept_low[...].astype(F32) + other_low[...].astype(F32)).astype(BF16)

        def kernel(last):
            return pl.pallas_call(
                body,
                grid_spec=pltpu.PrefetchScalarGridSpec(
                    num_scalar_prefetch=1,
                    grid=(grid,),
                    in_specs=[upper, lower, upper, lower, ANY],
                    out_specs=(straight, straight),
                ),
                out_shape=(
                    jax.ShapeDtypeStruct((half,) + kept.shape[1:], F32),
                    jax.ShapeDtypeStruct((half,) + kept.shape[1:], BF16),
                ),
                compiler_params=params(24),
                cost_estimate=cost(self.length()),
                name="halve",
            )(self.place, kept, kept, other, other, last)

        return self.run(kernel)

    def reduce(self, parts, first, last):
        for at in list(range(len(self.steps)))[::-1][first:last]:
            kept, low = self.halve(at, *parts)
            parts = kept, self.swap(low, *self.steps[at])
        return parts


def settle(parts):
    return parts[0][0].astype(F32) + parts[1][0].astype(F32)


def collect(into, rows, slots, core, held, other):
    for place, (parity, piece) in enumerate(slots):
        mine = held(piece)
        theirs = other(piece)
        first, second = (mine, theirs) if parity == 0 else (theirs, mine)
        into[place * rows : (place + 1) * rows, :] = jnp.where(core == 0, first, second)


def deal(values, rows, slots, core, kept, sent):
    halves = ({}, {})
    for place, (parity, piece) in enumerate(slots):
        halves[parity][piece] = values[place * rows : (place + 1) * rows, :]
    for piece, even in halves[0].items():
        odd = halves[1][piece]
        kept(piece, jnp.where(core == 0, even, odd))
        sent(piece, jnp.where(core == 0, odd, even))


def standard(values):
    centred = values - jnp.mean(values, axis=-1, keepdims=True)
    rate = lax.rsqrt(jnp.mean(centred * centred, axis=-1, keepdims=True) + 1e-06)
    return centred * rate, rate


def standard_back(grad, gain, standardised, rate):
    pushed = grad * gain
    along = jnp.mean(pushed * standardised, axis=-1, keepdims=True)
    inner = pushed - jnp.mean(pushed, axis=-1, keepdims=True) - standardised * along
    sums = (jnp.sum(grad * standardised, axis=0, keepdims=True), jnp.sum(grad, axis=0, keepdims=True))
    return (rate * inner,) + sums


def first_half(width):
    return lax.broadcasted_iota(jnp.int32, (SLOT, 2 * HEAD_DIM), 1) < HEAD_DIM


def line_up_kernel(*refs):
    *lines, bias, columns = refs
    rows = columns.shape[1]
    lines = [line[...].astype(F32).reshape(1, rows) for line in lines]
    bias = bias[...].astype(F32).reshape(1, -1)
    lines += [bias[:, at : at + rows] for at in range(0, bias.shape[1], rows)]
    lines.append(jnp.zeros((128 - len(lines), rows), F32))
    columns[0] = jnp.concatenate(lines, axis=0).T.astype(BF16)


def spread_kernel(images, live, block_in, cotangent, earlier, x_ref, dm_ref):
    for ref, into in ((block_in, x_ref), (cotangent, dm_ref)):
        values = ref[...].astype(F32)
        for image in range(images):
            part = values[image * LEN : (image + 1) * LEN]
            if into is dm_ref:
                part = jnp.where(live[image * LEN] != 0, part, 0.0)
            part = jnp.concatenate([part, jnp.zeros((SLOT - LEN, D), F32)], axis=0)
            into[image * SLOT : (image + 1) * SLOT, :] = part.astype(BF16)


def trim(values):
    parts = [values[at : at + LEN] for at in range(0, values.shape[0], SLOT)]
    return jnp.concatenate(parts, axis=0)


def join_kernel(*refs):
    *parts, earlier, out = refs
    start = 0
    for part in parts:
        out[0, :, start : start + part.shape[1]] = part[...]
        start += part.shape[1]


def attend_kernel(slots, rows, place, x_ref, held, other, earlier, normed, qkv, attended, lse, vec, weight, columns):
    core = place[0]
    collect(
        weight,
        rows,
        slots,
        core,
        lambda p: held[p[0], p[1], :, : 3 * D],
        lambda p: other[p[0], p[1], :, : 3 * D],
    )
    collect(
        columns,
        rows,
        slots,
        core,
        lambda p: held[p[0], p[1], :, 3 * D :],
        lambda p: other[p[0], p[1], :, 3 * D :],
    )
    vec[...] = columns[...].astype(F32).T[: vec.shape[0], :]
    shaped, _ = standard(x_ref[...].astype(F32))
    low = (shaped * vec[0:1, :] + vec[1:2, :]).astype(BF16)
    normed[...] = low
    for part, row in ((0, 2), (1, None), (2, 3)):
        cols = pl.ds(part * D, D)
        packed = mul(low, weight[:, cols])
        if row is not None:
            packed = packed + vec[row : row + 1, :]
        qkv[:, cols] = packed.astype(BF16)
    left = first_half(0)
    real = lax.broadcasted_iota(jnp.int32, (SLOT, SLOT), 1) < LEN
    lane = lax.broadcasted_iota(jnp.int32, (SLOT, 128), 1)
    images = x_ref.shape[0] // SLOT
    lse[...] = jnp.zeros_like(lse)

    def pair_step(at, carry):
        image, pair = at // (HEADS // 2), at % (HEADS // 2)
        tokens = pl.ds(pl.multiple_of(image * SLOT, 16), SLOT)
        cols = lambda part: pl.ds(pl.multiple_of(part * D + pair * 128, 128), 128)
        query, key, value = qkv[tokens, cols(0)], qkv[tokens, cols(1)], qkv[tokens, cols(2)]
        mixed, logs = [], lse[tokens, :]
        for side in range(2):
            chosen = left if side == 0 else ~left
            scores = mul_t(jnp.where(chosen, query, jnp.zeros_like(query)), key) * SCALE
            scores = jnp.where(real, scores, -1e30)
            top = jnp.max(scores, axis=-1, keepdims=True)
            raised = jnp.exp(scores - top)
            total = jnp.sum(raised, axis=-1, keepdims=True)
            logs = jnp.where(lane == pair * 2 + side, top + jnp.log(total), logs)
            mixed.append(mul((raised * (1.0 / total)).astype(BF16), value))
        lse[tokens, :] = logs
        attended[tokens, cols(0)] = jnp.where(left, mixed[0], mixed[1]).astype(BF16)
        return carry

    lax.fori_loop(0, images * (HEADS // 2), pair_step, 0)


def up_kernel(slots, plane_slots, rows, ff_rows, place, x_ref, attended, dm, held, other, vec, ubias, earlier, middle, normed, active, slope, kept, sent, weight):
    core = place[0]
    step = pl.program_id(0)
    collect(weight, rows, slots, core, lambda p: held[p[0], p[1]], lambda p: other[p[0], p[1]])

    @pl.when(step == 0)
    def _():
        total = x_ref[...].astype(F32) + mul(attended[...], weight[...]) + vec[4:5, :]
        middle[...] = total
        shaped, _ = standard(total)
        normed[...] = (shaped * vec[5:6, :] + vec[6:7, :]).astype(BF16)

    @pl.when(step > 0)
    def _():
        pre = mul(normed[...], weight[...]) + ubias[0:1, :]
        share = 0.5 + 0.5 * lax.erf(pre * (0.5**0.5))
        low = (pre * share).astype(BF16)
        active[...] = low
        slope[...] = share + pre * (jnp.exp(pre * pre * -0.5) * 0.3989422804014327)
        grad = t_mul(low, dm[...]).astype(BF16)

        def put(ref):
            def store(piece, value):
                ref[piece[0], 0] = value

            return store

        deal(grad, ff_rows, plane_slots, core, put(kept), put(sent))


def down_kernel(slots, plane_slots, rows, ff_rows, place, live, dm, middle, normed, attended, active, slope, held, other, dheld, dother, vec, earlier, dmid, datt, kept, sent, sums, usums, result, weight, dweight, mixed, back):
    core = place[0]
    step = pl.program_id(0)
    collect(weight, rows, slots, core, lambda p: held[p[0], p[1]], lambda p: other[p[0], p[1]])

    def put(ref):
        def store(piece, value):
            ref[piece[0], piece[1]] = value

        return store

    @pl.when(step < 4)
    def _():
        collect(dweight, ff_rows, plane_slots, core, lambda p: dheld[p[0], 0], lambda p: dother[p[0], 0])
        grad = mul_t(dm[...], dweight[...]) * slope[...]
        low = grad.astype(BF16)
        usums[...] = jnp.broadcast_to(jnp.sum(low.astype(F32), axis=0, keepdims=True), usums.shape)
        deal(t_mul(normed[...], low).astype(BF16), rows, slots, core, put(kept), put(sent))
        more = mul(active[...], dweight[...])
        turned = mul_t(low, weight[...])

        @pl.when(step == 0)
        def _():
            mixed[...] = more
            back[...] = turned

        @pl.when(step > 0)
        def _():
            mixed[...] += more
            back[...] += turned

    @pl.when(step == 4)
    def _():
        source = dm[...].astype(F32)
        full = middle[...] + mixed[...] + vec[7:8, :]
        keep = jnp.concatenate(
            [jnp.where(live[image * LEN] != 0, full[image * SLOT : image * SLOT + LEN], 0.0) for image in range(full.shape[0] // SLOT)],
            axis=0,
        )
        result[...] = keep.astype(BF16)
        shaped, rate = standard(middle[...])
        inner, ggain, gshift = standard_back(back[...], vec[5:6, :], shaped, rate)
        total = source + inner
        dmid[...] = total
        low = total.astype(BF16)
        datt[...] = mul_t(low, weight[...]).astype(BF16)
        deal(t_mul(attended[...], low).astype(BF16), rows, slots, core, put(kept), put(sent))
        gout = jnp.sum(low.astype(F32), axis=0, keepdims=True)
        gdown = jnp.sum(source, axis=0, keepdims=True)
        sums[...] = jnp.concatenate([gout, ggain, gshift, gdown] * 2, axis=0)


def heads_kernel(qkv, datt, lse, earlier, dqkv):
    left = first_half(0)
    real = lax.broadcasted_iota(jnp.int32, (SLOT, SLOT), 1) < LEN
    lane = lax.broadcasted_iota(jnp.int32, (SLOT, 128), 1)
    logs = lse[...]

    def pair_step(pair, carry):
        cols = lambda part: pl.ds(pl.multiple_of(part * D + pair * 128, 128), 128)
        query, key, value = qkv[:, cols(0)], qkv[:, cols(1)], qkv[:, cols(2)]
        grad = datt[:, cols(0)]
        dq, dk, dv = [], [], []
        for side in range(2):
            chosen = left if side == 0 else ~left
            scores = mul_t(jnp.where(chosen, query, jnp.zeros_like(query)), key) * SCALE
            log = jnp.sum(jnp.where(lane == pair * 2 + side, logs, 0.0), axis=-1, keepdims=True)
            attn = jnp.where(real, jnp.exp(scores - log), 0.0)
            dattn = mul_t(jnp.where(chosen, grad, jnp.zeros_like(grad)), value)
            dscores = (attn * (dattn - jnp.sum(attn * dattn, axis=-1, keepdims=True))).astype(BF16)
            dv.append(t_mul(attn.astype(BF16), grad))
            dq.append(mul(dscores, key) * SCALE)
            dk.append(t_mul(dscores, query) * SCALE)
        for part, halves in ((0, dq), (1, dk), (2, dv)):
            dqkv[:, cols(part)] = jnp.where(left, halves[0], halves[1]).astype(BF16)
        return carry

    lax.fori_loop(0, HEADS // 2, pair_step, 0)


def input_kernel(slots, rows, images, place, x_ref, dmid, normed, *refs):
    dqkv, (held, other, vec, sums, usums, earlier, kept, sent, igrad, weight) = refs[:images], refs[images:]
    core = place[0]
    collect(
        weight,
        rows,
        slots,
        core,
        lambda p: held[p[0], p[1], :, : 3 * D],
        lambda p: other[p[0], p[1], :, : 3 * D],
    )

    def put(ref, cols):
        def store(piece, value):
            ref[piece[0], piece[1], :, cols] = value

        return store

    back = None
    rowsums = []
    for part in range(3):
        cols = pl.ds(part * D, D)
        low = jnp.concatenate([ref[:, cols] for ref in dqkv], axis=0)
        rowsums.append(jnp.sum(low.astype(F32), axis=0, keepdims=True))
        grad = t_mul(normed[...], low).astype(BF16)
        deal(grad, rows, slots, core, put(kept, cols), put(sent, cols))
        more = mul_t(low, weight[:, cols])
        back = more if back is None else back + more
    shaped, rate = standard(x_ref[...].astype(F32))
    inner, ggain, gshift = standard_back(back, vec[0:1, :], shaped, rate)
    igrad[...] = trim(dmid[...] + inner)
    lines = [ggain, gshift, rowsums[0], rowsums[2], sums[0:4, :], usums[0:4, :]]
    lines.append(jnp.zeros((128 - 12, D), F32))
    columns = jnp.concatenate(lines, axis=0).T.astype(BF16)
    cols = pl.ds(3 * D, 128)
    deal(columns, rows, slots, core, put(kept, cols), put(sent, cols))


def shards(
    block_in,
    slot_mask,
    gain_first,
    shift_first,
    packed_weight,
    query_bias,
    value_bias,
    out_weight,
    out_bias,
    gain_second,
    shift_second,
    up_weight,
    up_bias,
    down_weight,
    down_bias,
    cotangent,
):
    links = Links(lax.axis_size("dp"))
    rows = packed_weight.shape[0]
    ff_rows = down_weight.shape[0]
    wide = ff_rows // rows
    count, plane, depth = links.count, links.plane, links.z
    slots = tuple((i % 2, links.slot(i)) for i in range(count))
    per_plane = count // depth
    plane_slots = slots[:per_plane]
    place = links.place
    tokens = block_in.shape[0]
    images = tokens // LEN
    size = images * SLOT
    shape = jax.ShapeDtypeStruct
    steps_z = depth.bit_length() - 1
    final = len(links.steps)

    gather_a = packed_weight[None]
    came_a = links.swap(gather_a, *links.steps[0])
    vectors = (gain_first, shift_first, query_bias, value_bias, out_bias, gain_second, shift_second, down_bias, up_bias)
    line_up = pl.pallas_call(
        line_up_kernel,
        out_shape=shape((1, rows, 128), BF16),
        in_specs=[VMEM] * 9,
        out_specs=VMEM,
        cost_estimate=cost(links.length()),
        name="line_up",
    )
    columns = links.run(lambda last: line_up(*vectors))
    came_v = links.swap(columns, *links.steps[0])
    x, dm = links.run(
        lambda last: pl.pallas_call(
            functools.partial(spread_kernel, images),
            out_shape=(shape((size, D), BF16), shape((size, D), BF16)),
            in_specs=[SMEM, VMEM, VMEM, ANY],
            out_specs=(VMEM, VMEM),
            compiler_params=pltpu.CompilerParams(vmem_limit_bytes=16 << 20),
            cost_estimate=cost(links.length()),
            name="spread",
        )(slot_mask, block_in, cotangent, last)
    )

    def joined(*parts):
        width = sum(part.shape[1] for part in parts)
        return links.run(
            lambda last: pl.pallas_call(
                join_kernel,
                out_shape=shape((1, parts[0].shape[0], width), BF16),
                in_specs=[VMEM] * len(parts) + [ANY],
                out_specs=VMEM,
                cost_estimate=cost(links.length()),
                name="join",
            )(*parts, last)
        )

    gather_a = links.pair(0, (gather_a, came_a))
    gather_b = joined(out_weight, up_weight)
    columns = links.pair(0, (columns, came_v))
    if steps_z > 2:
        gather_a = links.advance(gather_a, 1, steps_z - 1)
        columns = links.advance(columns, 1, steps_z - 1)
    at = steps_z - 1
    came_a, came_v = links.swap(gather_a, *links.steps[at]), links.swap(columns, *links.steps[at])
    came_b = links.swap(gather_b, *links.steps[0])
    gather_a = links.pair(at, (gather_a, came_a), (columns, came_v))
    gather_b = links.pair(0, (gather_b, came_b))
    gather_c = joined(down_weight)
    gather_a = links.advance(gather_a, steps_z, final - 1)
    gather_b = links.advance(gather_b, 1, steps_z)
    gather_c = links.advance(gather_c, 0, 1)
    held_a, other_a = links.across(links.advance(gather_a, final - 1, final))
    gather_b = links.advance(gather_b, steps_z, final - 1)
    gather_c = links.advance(gather_c, 1, steps_z)

    wide_a = 3 * D + 128
    normed, qkv, attended, lse, vec = links.run(
        lambda last: pl.pallas_call(
            functools.partial(attend_kernel, slots, rows),
            out_shape=(
                shape((size, D), BF16),
                shape((size, 3 * D), BF16),
                shape((size, D), BF16),
                shape((size, 128), F32),
                shape((16, D), F32),
            ),
            in_specs=[SMEM] + [VMEM] * 3 + [ANY],
            out_specs=(VMEM,) * 5,
            scratch_shapes=[pltpu.VMEM((D, 3 * D), BF16), pltpu.VMEM((D, 128), BF16)],
            compiler_params=pltpu.CompilerParams(vmem_limit_bytes=32 << 20),
            cost_estimate=cost(links.length()),
            name="attend",
        )(place, x, held_a, other_a, last)
    )
    ubias = vec[8 : 8 + wide].reshape(wide, count, rows).transpose(1, 0, 2).reshape(1, FF)
    gather_c = links.advance(gather_c, steps_z, final - 1)
    held_b, other_b = links.across(links.advance(gather_b, final - 1, final))

    fixed = lambda height, width: pl.BlockSpec((height, width), lambda t: (0, 0))
    z_place = lambda t: jnp.where(depth == 4, (t % 2) * 2 + t // 2, t)
    tile = FF // depth
    steps = depth + 1

    before = lambda t: jnp.maximum(t - 1, 0)
    block_b = pl.BlockSpec((plane, depth, rows, D), lambda t: (0, 0, 0, t))
    tiled = lambda height, at: pl.BlockSpec((height, tile), lambda t: (0, at(t)))
    dealt = pl.BlockSpec((plane, 1, ff_rows, D), lambda t: (0, z_place(before(t)), 0, 0))
    middle, normed_two, active, slope, kept_c, sent_c = links.run(
        lambda last: pl.pallas_call(
            functools.partial(up_kernel, slots, plane_slots, rows, ff_rows),
            grid=(steps,),
            out_shape=(
                shape((size, D), F32),
                shape((size, D), BF16),
                shape((size, FF), BF16),
                shape((size, FF), F32),
                shape((plane, depth, ff_rows, D), BF16),
                shape((plane, depth, ff_rows, D), BF16),
            ),
            in_specs=[SMEM] + [fixed(size, D)] * 3 + [block_b, block_b, fixed(16, D), tiled(1, before), ANY],
            out_specs=(fixed(size, D), fixed(size, D), tiled(size, before), tiled(size, before), dealt, dealt),
            scratch_shapes=[pltpu.VMEM((D, D), BF16)],
            compiler_params=params(32),
            cost_estimate=cost(links.length()),
            name="up",
        )(place, x, attended, dm, held_b, other_b, vec, ubias, last)
    )
    held_c, other_c = links.across(links.advance(gather_c, final - 1, final))
    parts_c = links.exchange(kept_c, sent_c)
    parts_c = links.reduce(parts_c, 0, 1)

    upto = lambda t: jnp.minimum(t, depth - 1)
    block_b = pl.BlockSpec((plane, depth, rows, D), lambda t: (0, 0, 0, (t + 1) % steps))
    block_c = pl.BlockSpec((plane, 1, ff_rows, D), lambda t: (0, z_place(upto(t)), 0, 0))
    dmid, datt, kept_b, sent_b, sums, usums, block_out = links.run(
        lambda last: pl.pallas_call(
            functools.partial(down_kernel, slots, plane_slots, rows, ff_rows),
            grid=(steps,),
            out_shape=(
                shape((size, D), F32),
                shape((size, D), BF16),
                shape((plane, depth, rows, D + FF), BF16),
                shape((plane, depth, rows, D + FF), BF16),
                shape((8, D), F32),
                shape((8, FF), F32),
                shape((tokens, D), BF16),
            ),
            in_specs=[SMEM, SMEM]
            + [fixed(size, D)] * 4
            + [tiled(size, upto), tiled(size, upto), block_b, block_b, block_c, block_c, fixed(16, D), ANY],
            out_specs=(
                fixed(size, D),
                fixed(size, D),
                block_b,
                block_b,
                fixed(8, D),
                tiled(8, upto),
                fixed(tokens, D),
            ),
            scratch_shapes=[
                pltpu.VMEM((D, D), BF16),
                pltpu.VMEM((D, D), BF16),
                pltpu.VMEM((size, D), F32),
                pltpu.VMEM((size, D), F32),
            ],
            compiler_params=params(40),
            cost_estimate=cost(links.length()),
            name="down",
        )(
            place,
            slot_mask,
            dm,
            middle,
            normed_two,
            attended,
            active,
            slope,
            held_b,
            other_b,
            held_c,
            other_c,
            vec,
            last,
        )
    )
    parts_b = links.exchange(kept_b, sent_b)
    parts_c = links.reduce(parts_c, 1, final - 2)
    usums = usums[0].reshape(count, wide, rows).transpose(1, 0, 2).reshape(wide, D)
    usums = jnp.pad(usums, ((0, 8 - wide), (0, 0)))

    def heads(image):
        row = lambda width: pl.BlockSpec((SLOT, width), lambda i: (image, 0))
        return links.run(
            lambda last: pl.pallas_call(
                heads_kernel,
                grid=(1,),
                out_shape=shape((SLOT, 3 * D), BF16),
                in_specs=[row(3 * D), row(D), row(128), ANY],
                out_specs=pl.BlockSpec((SLOT, 3 * D), lambda i: (0, 0)),
                compiler_params=params(16),
                cost_estimate=cost(links.length()),
                name="heads",
            )(qkv, datt, lse, last)
        )

    dqkv = [heads(0)]
    parts_b = links.reduce(parts_b, 0, 1)
    dqkv += [heads(image) for image in range(1, images)]
    parts_c = links.reduce(parts_c, final - 2, final - 1)
    kept_a, sent_a, igrad = links.run(
        lambda last: pl.pallas_call(
            functools.partial(input_kernel, slots, rows, images),
            out_shape=(
                shape((plane, depth, rows, wide_a), BF16),
                shape((plane, depth, rows, wide_a), BF16),
                shape((tokens, D), F32),
            ),
            in_specs=[SMEM] + [VMEM] * (8 + images) + [ANY],
            out_specs=(VMEM,) * 3,
            scratch_shapes=[pltpu.VMEM((D, 3 * D), BF16)],
            compiler_params=pltpu.CompilerParams(vmem_limit_bytes=36 << 20),
            cost_estimate=cost(links.length()),
            name="inward",
        )(place, x, dmid, normed, *dqkv, held_a, other_a, vec, sums, usums, last)
    )
    parts_a = links.exchange(kept_a, sent_a)
    parts_b = links.reduce(parts_b, 1, final - 2)
    parts_c = links.reduce(parts_c, final - 1, final)
    parts_a = links.reduce(parts_a, 0, 1)
    parts_b = links.reduce(parts_b, final - 2, final - 1)
    parts_a = links.reduce(parts_a, 1, final - 2)
    parts_b = links.reduce(parts_b, final - 1, final)
    parts_a = links.reduce(parts_a, final - 2, final)
    grads_a, grads_b, grad_down_weight = settle(parts_a), settle(parts_b), settle(parts_c)
    small = grads_a[:, 3 * D : 3 * D + 8 + wide].T
    return (
        block_out,
        igrad,
        small[0],
        small[1],
        grads_a[:, : 3 * D],
        small[2],
        small[3],
        grads_b[:, :D],
        small[4],
        small[5],
        small[6],
        grads_b[:, D:],
        small[8:].reshape(-1),
        grad_down_weight,
        small[7],
    )


def solution(mesh):
    row, flat = P("dp", None), P("dp")
    in_specs = (row, flat, flat, flat, row, flat, flat, row, flat, flat, flat, row, flat, row, flat, row)
    out_specs = (row, row, flat, flat, row, flat, flat, row, flat, flat, flat, row, flat, row, flat)
    return jax.shard_map(shards, mesh=mesh, in_specs=in_specs, out_specs=out_specs, check_vma=False)
```

```python
import functools

import jax
import jax.numpy as jnp
from jax import lax
from jax.experimental import pallas as pl
from jax.experimental.pallas import tpu as pltpu
from jax.sharding import PartitionSpec as P

D = 768
HEADS = 12
HEAD_DIM = 64
FF = 3072
LEN = 197
SLOT = 208
SPEED = 1.15e9
LENGTHS = (12, 0.25, 0.25, 1, 1, 0.5, 12, 1, 0.25, 24, 0.25, 0.25, 16, 6, 16, 0.25, 16, 3, 0.5, 0.25, 16, 6, 3, 2, 8, 0.5, 6, 2, 2, 6, 1, 1, 24, 0.5, 0.25, 1, 3, 32, 0.25, 0.25, 2, 0.5, 0.5, 0.25)
ORDERS = {'a': 'fnxx', 'b': 'nxfx', 'e': 'fxnx', 'c': 'fxxn', 'd': 'xxnf', 'u': 'xxnf', 'i': 'xxnf', 'j': 'xxfn'}
GATHERS = ("a", "b", "e", "c")
FIRST = 2
PINNED = {}
SCALE = HEAD_DIM ** (-0.5)
F32 = jnp.float32
BF16 = jnp.bfloat16
VMEM = pl.BlockSpec(memory_space=pltpu.VMEM)
SMEM = pl.BlockSpec(memory_space=pltpu.SMEM)
ANY = pl.BlockSpec(memory_space=pl.ANY)
TOKEN = pltpu.HBM((8, 128), F32)


def params(megabytes):
    return pltpu.CompilerParams(
        vmem_limit_bytes=megabytes << 20, dimension_semantics=("arbitrary",)
    )


def cost(length):
    return pl.CostEstimate(flops=int(length * SPEED), transcendentals=0, bytes_accessed=D)


def mul(a, b):
    return jnp.dot(a, b, preferred_element_type=F32)


def mul_t(a, b):
    return lax.dot_general(a, b, (((1,), (1,)), ((), ())), preferred_element_type=F32)


def t_mul(a, b):
    return lax.dot_general(a, b, (((0,), (0,)), ((), ())), preferred_element_type=F32)


class Links:
    def __init__(self, count):
        chips = count // 2
        z = min(4, chips)
        plane = chips // z
        x = 1
        while x * x < plane:
            x *= 2
        self.count, self.z, self.plane = count, z, plane
        bit = 2
        x_bits, y_bits, z_bits = [], [], []
        for bits, extent in ((x_bits, x), (y_bits, plane // x), (z_bits, z)):
            size = 1
            while size < extent:
                bits.append(bit)
                bit *= 2
                size *= 2
        across = list(zip(x_bits + y_bits, y_bits + x_bits))
        half = (len(across) + 1) // 2
        self.near = [(b, b) for b in z_bits[:1]]
        self.far = [(b, b) for b in z_bits[1:]]
        self.across = across[:half], across[half:]
        self.all = self.near + self.far + across
        index = lax.axis_index("dp")
        core = index % 2
        sides = [((index & jnp.where(core == 0, *step)) != 0).astype(jnp.int32) for step in self.all]
        self.place = jnp.stack([core.astype(jnp.int32)] + sides)
        self.last = None
        self.lengths = iter(LENGTHS + (1,) * 64)

    def length(self):
        return next(self.lengths)

    def hops(self, order):
        found, crossed = [], 0
        for kind in order:
            if kind == "x":
                found.append(self.across[crossed])
                crossed += 1
            else:
                found.append(self.far if kind == "f" else self.near)
        return found

    def steps(self, order, scatter):
        steps = [step for hop in self.hops(order) for step in hop]
        return steps[::-1] if scatter else steps

    def slots(self, order, scatter):
        steps = self.steps(order, scatter)
        found = []
        for device in range(self.count):
            bits = [1 if device & step[device % 2] else 0 for step in steps]
            found.append((device % 2, sum(b << weight for weight, b in enumerate(bits))))
        return tuple(found)

    def tiles(self, order, scatter):
        steps = self.steps(order, scatter)[::-1]
        along = [step in self.near or step in self.far for step in steps]
        block = tuple(1 if z else 2 for z in along)

        def index(t):
            return tuple((t % 2 if step in self.near else t // 2) if z else 0 for step, z in zip(steps, along))

        found = []
        for device in range(self.count // self.z):
            found.append((device % 2, tuple(1 if device & step[device % 2] else 0 for step in steps)))
        return (2,) * len(steps), block, index, tuple(found)

    def run(self, kernel, *args, **options):
        *out, self.last = kernel(self.last, *args, **options)
        return tuple(out)

    def swap(self, value, even, odd):
        pairs = [(i, i ^ (odd if i % 2 else even)) for i in range(self.count)]
        return lax.ppermute(value, "dp", pairs)

    def pair(self, step, held, other):
        count, rows, width = held.shape
        at = self.all.index(step)

        def body(place, held, other, *refs):
            out = refs[-2]
            high = place[1 + at]

            def copy(i, carry):
                out[high, i] = held[i]
                out[1 - high, i] = other[i]
                return carry

            lax.fori_loop(0, count, copy, 0)

        def kernel(last):
            return pl.pallas_call(
                body,
                out_shape=(jax.ShapeDtypeStruct((2, count, rows, width), BF16), TOKEN),
                in_specs=[SMEM, VMEM, VMEM] + ([] if last is None else [ANY]),
                out_specs=(VMEM, ANY),
                compiler_params=pltpu.CompilerParams(vmem_limit_bytes=10 << 20),
                cost_estimate=cost(self.length()),
                name="pair",
            )(self.place, held, other, *([] if last is None else [pinned(last)]))

        return self.run(kernel)[0].reshape(2 * count, rows, width)

    def advance(self, held, hop):
        for step in hop:
            held = self.pair(step, held, self.swap(held, *step))
        return held

    def exchange(self, kept, sent):
        other = self.swap(sent, 1, 1)
        shape = (-1,) + kept.shape[-2:]
        return kept.reshape(shape), other.reshape(shape)

    def halve(self, step, kept, other):
        at = self.all.index(step)
        half = kept.shape[0] // 2
        chunk = max(1, half // 4)
        grid = half // chunk
        block = (chunk,) + kept.shape[1:]
        upper = pl.BlockSpec(block, lambda i, place: (place[1 + at] * grid + i, 0, 0))
        lower = pl.BlockSpec(block, lambda i, place: ((1 - place[1 + at]) * grid + i, 0, 0))
        straight = pl.BlockSpec(block, lambda i, place: (i, 0, 0))

        def body(place, kept_up, kept_low, other_up, other_low, last, stay, leave, token):
            stay[...] = kept_up[...].astype(F32) + other_up[...].astype(F32)
            leave[...] = (kept_low[...].astype(F32) + other_low[...].astype(F32)).astype(BF16)

        def kernel(last):
            return pl.pallas_call(
                body,
                grid_spec=pltpu.PrefetchScalarGridSpec(
                    num_scalar_prefetch=1,
                    grid=(grid,),
                    in_specs=[upper, lower, upper, lower, ANY],
                    out_specs=(straight, straight, ANY),
                ),
                out_shape=(
                    jax.ShapeDtypeStruct((half,) + kept.shape[1:], F32),
                    jax.ShapeDtypeStruct((half,) + kept.shape[1:], BF16),
                    TOKEN,
                ),
                compiler_params=params(12),
                cost_estimate=cost(self.length()),
                name="halve",
            )(self.place, kept, kept, other, other, pinned(last))

        return self.run(kernel)

    def reduce(self, parts, hop):
        for step in hop:
            kept, low = self.halve(step, *parts)
            parts = kept, self.swap(low, *step)
        return parts


def pinned(value):
    return pltpu.with_memory_space_constraint(value, pltpu.HBM)


def settle(parts):
    return parts[0][0].astype(F32) + parts[1][0].astype(F32)


def collect(into, rows, slots, core, held, other, cols=slice(None)):
    @pl.when(core == 0)
    def _():
        for place, (parity, piece) in enumerate(slots):
            source = other if parity else held
            into[place * rows : (place + 1) * rows, :] = source[piece + (slice(None), cols)]

    @pl.when(core == 1)
    def _():
        for place, (parity, piece) in enumerate(slots):
            source = held if parity else other
            into[place * rows : (place + 1) * rows, :] = source[piece + (slice(None), cols)]


def deal(values, rows, slots, core, kept, sent, cols=slice(None)):
    halves = ({}, {})
    for place, (parity, piece) in enumerate(slots):
        halves[parity][piece] = values[place * rows : (place + 1) * rows, :]
    for piece, even in halves[0].items():
        odd = halves[1][piece]
        kept[piece + (slice(None), cols)] = jnp.where(core == 0, even, odd)
        sent[piece + (slice(None), cols)] = jnp.where(core == 0, odd, even)


def standard(values):
    centred = values - jnp.mean(values, axis=-1, keepdims=True)
    rate = lax.rsqrt(jnp.mean(centred * centred, axis=-1, keepdims=True) + 1e-06)
    return centred * rate, rate


def standard_back(grad, gain, standardised, rate):
    pushed = grad * gain
    along = jnp.mean(pushed * standardised, axis=-1, keepdims=True)
    inner = pushed - jnp.mean(pushed, axis=-1, keepdims=True) - standardised * along
    sums = (jnp.sum(grad * standardised, axis=0, keepdims=True), jnp.sum(grad, axis=0, keepdims=True))
    return (rate * inner,) + sums


def first_half(width):
    return lax.broadcasted_iota(jnp.int32, (SLOT, 2 * HEAD_DIM), 1) < HEAD_DIM


def line_up_kernel(weight, *refs):
    lines, bias, out = refs[:8], refs[8], refs[-1]
    rows = weight.shape[0]
    out[0, :, : 3 * D] = weight[...]
    lines = [line[...].astype(F32).reshape(1, rows) for line in lines]
    bias = bias[...].astype(F32).reshape(1, -1)
    lines += [bias[:, at : at + rows] for at in range(0, bias.shape[1], rows)]
    lines.append(jnp.zeros((128 - len(lines), rows), F32))
    out[0, :, 3 * D :] = jnp.concatenate(lines, axis=0).T.astype(BF16)


def spread_kernel(images, live, block_in, cotangent, earlier, x_ref, dm_ref):
    for ref, into in ((block_in, x_ref), (cotangent, dm_ref)):
        values = ref[...].astype(F32)
        for image in range(images):
            part = values[image * LEN : (image + 1) * LEN]
            if into is dm_ref:
                part = jnp.where(live[image * LEN] != 0, part, 0.0)
            part = jnp.concatenate([part, jnp.zeros((SLOT - LEN, D), F32)], axis=0)
            into[image * SLOT : (image + 1) * SLOT, :] = part.astype(BF16)


def trim(values):
    parts = [values[at : at + LEN] for at in range(0, values.shape[0], SLOT)]
    return jnp.concatenate(parts, axis=0)


def join_kernel(ranges, *refs):
    out = refs[-1]
    start = 0
    for part, (first, last) in zip(refs, ranges):
        out[0, :, start : start + last - first] = part[:, first:last]
        start += last - first


def attend_kernel(slots, rows, place, x_ref, held, other, earlier, normed, qkv, attended, lse, vec, weight, columns):
    core = place[0]
    collect(weight, rows, slots, core, held, other, slice(0, 3 * D))
    collect(columns, rows, slots, core, held, other, slice(3 * D, 3 * D + 128))
    vec[...] = columns[...].astype(F32).T[: vec.shape[0], :]
    shaped, _ = standard(x_ref[...].astype(F32))
    low = (shaped * vec[0:1, :] + vec[1:2, :]).astype(BF16)
    normed[...] = low
    for part, row in ((0, 2), (1, None), (2, 3)):
        cols = pl.ds(part * D, D)
        packed = mul(low, weight[:, cols])
        if row is not None:
            packed = packed + vec[row : row + 1, :]
        qkv[:, cols] = packed.astype(BF16)
    left = first_half(0)
    real = lax.broadcasted_iota(jnp.int32, (SLOT, SLOT), 1) < LEN
    lane = lax.broadcasted_iota(jnp.int32, (SLOT, 128), 1)
    images = x_ref.shape[0] // SLOT
    lse[...] = jnp.zeros_like(lse)

    def pair_step(at, carry):
        image, pair = at // (HEADS // 2), at % (HEADS // 2)
        tokens = pl.ds(pl.multiple_of(image * SLOT, 16), SLOT)
        cols = lambda part: pl.ds(pl.multiple_of(part * D + pair * 128, 128), 128)
        query, key, value = qkv[tokens, cols(0)], qkv[tokens, cols(1)], qkv[tokens, cols(2)]
        mixed, logs = [], lse[tokens, :]
        for side in range(2):
            chosen = left if side == 0 else ~left
            scores = mul_t(jnp.where(chosen, query, jnp.zeros_like(query)), key) * SCALE
            scores = jnp.where(real, scores, -1e30)
            top = jnp.max(scores, axis=-1, keepdims=True)
            raised = jnp.exp(scores - top)
            total = jnp.sum(raised, axis=-1, keepdims=True)
            logs = jnp.where(lane == pair * 2 + side, top + jnp.log(total), logs)
            mixed.append(mul((raised * (1.0 / total)).astype(BF16), value))
        lse[tokens, :] = logs
        attended[tokens, cols(0)] = jnp.where(left, mixed[0], mixed[1]).astype(BF16)
        return carry

    lax.fori_loop(0, images * (HEADS // 2), pair_step, 0, unroll=HEADS // 2)


def up_kernel(slots_b, slots_e, slots_d, rows, ff_rows, place, x_ref, attended, dm, held, other, held_e, other_e, vec, ubias, earlier, middle, normed, active, slope, kept, sent, weight):
    core = place[0]
    step = pl.program_id(0)

    @pl.when(step <= FIRST)
    def _():
        collect(weight, rows, slots_b, core, held, other)

    @pl.when(step > FIRST)
    def _():
        collect(weight, rows, slots_e, core, held_e, other_e)

    @pl.when(step == 0)
    def _():
        total = x_ref[...].astype(F32) + mul(attended[...], weight[...]) + vec[4:5, :]
        middle[...] = total
        shaped, _ = standard(total)
        normed[...] = (shaped * vec[5:6, :] + vec[6:7, :]).astype(BF16)

    @pl.when(step > 0)
    def _():
        pre = mul(normed[...], weight[...]) + ubias[0:1, :]
        share = 0.5 + 0.5 * lax.erf(pre * (0.5**0.5))
        low = (pre * share).astype(BF16)
        active[...] = low
        slope[...] = share + pre * (jnp.exp(pre * pre * -0.5) * 0.3989422804014327)
        grad = t_mul(low, dm[...]).astype(BF16)

        deal(grad, ff_rows, slots_d, core, kept, sent)


def slope_kernel(slots_u, slots_c, rows, ff_rows, place, dm, normed, slope, held, other, earlier, low, kept, sent, sums, weight):
    core = place[0]
    collect(weight, ff_rows, slots_c, core, held, other)
    grad = (mul_t(dm[...], weight[...]) * slope[...]).astype(BF16)
    low[...] = grad
    deal(t_mul(normed[...], grad).astype(BF16), rows, slots_u, core, kept, sent)
    lines = jnp.broadcast_to(jnp.sum(grad.astype(F32), axis=0, keepdims=True), (128, grad.shape[1])).T
    lane = lax.broadcasted_iota(jnp.int32, (rows, 128), 1)
    for device in range(grad.shape[1] // ff_rows):
        total = jnp.zeros((rows, 128), F32)
        for at in range(ff_rows // rows):
            start = device * ff_rows + at * rows
            total = jnp.where(lane == 8 + at, lines[start : start + rows, :], total)
        sums[device * rows : (device + 1) * rows, :] = total


def middle_kernel(slots_b, slots_e, slots_i, rows, place, low, middle, dm, attended, held, other, held_e, other_e, vec, earlier, datt, dmid, kept, sent, sums, weight, back):
    core = place[0]
    step = pl.program_id(0)
    last = pl.num_programs(0) - 1

    @pl.when((step < FIRST) | (step == last))
    def _():
        collect(weight, rows, slots_b, core, held, other)

    @pl.when((step >= FIRST) & (step < last))
    def _():
        collect(weight, rows, slots_e, core, held_e, other_e)

    @pl.when(step == 0)
    def _():
        back[...] = mul_t(low[...], weight[...])

    @pl.when((step > 0) & (step < last))
    def _():
        back[...] += mul_t(low[...], weight[...])

    @pl.when(step == last)
    def _():
        source = dm[...].astype(F32)
        shaped, rate = standard(middle[...])
        inner, ggain, gshift = standard_back(back[...], vec[5:6, :], shaped, rate)
        total = source + inner
        dmid[...] = total
        branch = total.astype(BF16)
        datt[...] = mul_t(branch, weight[...]).astype(BF16)
        deal(t_mul(attended[...], branch).astype(BF16), rows, slots_i, core, kept, sent)
        gout = jnp.sum(branch.astype(F32), axis=0, keepdims=True)
        gdown = jnp.sum(source, axis=0, keepdims=True)
        sums[...] = jnp.concatenate([gout, ggain, gshift, gdown] * 2, axis=0)


def down_kernel(slots_c, ff_rows, place, live, active, middle, held, other, vec, earlier, result, weight, mixed):
    core = place[0]
    step = pl.program_id(0)
    collect(weight, ff_rows, slots_c, core, held, other)
    more = mul(active[...], weight[...])

    @pl.when(step == 0)
    def _():
        mixed[...] = more

    @pl.when(step > 0)
    def _():
        mixed[...] += more

    @pl.when(step == pl.num_programs(0) - 1)
    def _():
        full = middle[...] + mixed[...] + vec[7:8, :]
        images = full.shape[0] // SLOT
        keep = [jnp.where(live[i * LEN] != 0, full[i * SLOT : i * SLOT + LEN], 0.0) for i in range(images)]
        result[...] = jnp.concatenate(keep, axis=0).astype(BF16)


def heads_kernel(slots, rows, first, beside, place, qkv, datt, lse, normed, *refs):
    more, (earlier, dqkv, kept, sent) = refs[:-4], refs[-4:]
    core = place[0]
    left = first_half(0)
    real = lax.broadcasted_iota(jnp.int32, (SLOT, SLOT), 1) < LEN
    lane = lax.broadcasted_iota(jnp.int32, (SLOT, 128), 1)
    pairs = HEADS // 4
    images = qkv.shape[0] // SLOT
    for source, into in zip(more, (kept, sent)):
        into[:, :, :beside] = source[...]

    def pair_step(at, carry):
        image, local = at // pairs, at % pairs
        pair = first + local
        tokens = pl.ds(pl.multiple_of(image * SLOT, 16), SLOT)
        cols = lambda part: pl.ds(pl.multiple_of(part * D + pair * 128, 128), 128)
        query, key, value = qkv[tokens, cols(0)], qkv[tokens, cols(1)], qkv[tokens, cols(2)]
        grad, logs = datt[tokens, cols(0)], lse[tokens, :]
        dq, dk, dv = [], [], []
        for side in range(2):
            chosen = left if side == 0 else ~left
            scores = mul_t(jnp.where(chosen, query, jnp.zeros_like(query)), key) * SCALE
            log = jnp.sum(jnp.where(lane == pair * 2 + side, logs, 0.0), axis=-1, keepdims=True)
            attn = jnp.where(real, jnp.exp(scores - log), 0.0)
            dattn = mul_t(jnp.where(chosen, grad, jnp.zeros_like(grad)), value)
            dscores = (attn * (dattn - jnp.sum(attn * dattn, axis=-1, keepdims=True))).astype(BF16)
            dv.append(t_mul(attn.astype(BF16), grad))
            dq.append(mul(dscores, key) * SCALE)
            dk.append(t_mul(dscores, query) * SCALE)
        for part, halves in ((0, dq), (1, dk), (2, dv)):
            into = pl.ds(pl.multiple_of(part * (D // 2) + local * 128, 128), 128)
            dqkv[tokens, into] = jnp.where(left, halves[0], halves[1]).astype(BF16)
        return carry

    lax.fori_loop(0, images * pairs, pair_step, 0, unroll=images * pairs)
    grad = t_mul(normed[...], dqkv[...]).astype(BF16)
    deal(grad, rows, slots, core, kept, sent, slice(beside, beside + 3 * D // 2))


def input_kernel(slots_a, slots_j, rows, place, x_ref, dmid, half_a, half_b, kept_b, sent_b, held, other, vec, sums, usums, earlier, kept, sent, igrad, weight):
    core = place[0]
    for source, into in ((kept_b, kept), (sent_b, sent)):
        into[:, :, : source.shape[2]] = source[...]
    collect(weight, rows, slots_a, core, held, other, slice(0, 3 * D))
    back = None
    rowsums = []
    for part in range(3):
        cols = pl.ds(part * (D // 2), D // 2)
        low = jnp.concatenate([half_a[:, cols], half_b[:, cols]], axis=1)
        rowsums.append(jnp.sum(low.astype(F32), axis=0, keepdims=True))
        more = mul_t(low, weight[:, pl.ds(part * D, D)])
        back = more if back is None else back + more
    shaped, rate = standard(x_ref[...].astype(F32))
    inner, ggain, gshift = standard_back(back, vec[0:1, :], shaped, rate)
    igrad[...] = trim(dmid[...] + inner)
    lines = [ggain, gshift, rowsums[0], rowsums[2], sums[0:4, :]]
    lines.append(jnp.zeros((128 - 8, D), F32))
    columns = (jnp.concatenate(lines, axis=0).T + usums[...]).astype(BF16)
    deal(columns, rows, slots_j, core, kept, sent, slice(kept_b.shape[2], kept_b.shape[2] + 128))


def zeroed(piece, part):
    return tuple(0 if extent == 1 else bit for bit, extent in zip(piece, part))


def shards(
    block_in,
    slot_mask,
    gain_first,
    shift_first,
    packed_weight,
    query_bias,
    value_bias,
    out_weight,
    out_bias,
    gain_second,
    shift_second,
    up_weight,
    up_bias,
    down_weight,
    down_bias,
    cotangent,
):
    links = Links(lax.axis_size("dp"))
    rows = packed_weight.shape[0]
    ff_rows = down_weight.shape[0]
    wide = ff_rows // rows
    count, depth = links.count, links.z
    number = count // 2
    place = links.place
    tokens = block_in.shape[0]
    images = tokens // LEN
    size = images * SLOT
    hops = {group: links.hops(order) for group, order in ORDERS.items()}
    slots = {group: links.slots(order, group not in GATHERS) for group, order in ORDERS.items()}
    flat = {group: tuple((parity, (piece,)) for parity, piece in found) for group, found in slots.items()}
    shape = jax.ShapeDtypeStruct
    pieces = lambda cols: shape((number, rows, cols), BF16)
    fixed = lambda height, width: pl.BlockSpec((height, width), lambda t: (0, 0))
    tile = FF // depth
    tiled = lambda height, at: pl.BlockSpec((height, tile), lambda t: (0, at(t)))
    whole = lambda cols: pl.BlockSpec((number, rows, cols), lambda t: (0, 0, 0))
    before = lambda t: jnp.maximum(t - 1, 0)
    upto = lambda t: jnp.minimum(t, depth - 1)
    same = lambda t: t
    view_c, part_c, at_c, slots_c = links.tiles(ORDERS["c"], False)
    view_d, part_d, at_d, slots_d = links.tiles(ORDERS["d"], True)
    slots_c, slots_d = (tuple((parity, zeroed(piece, part)) for parity, piece in found) for found, part in ((slots_c, part_c), (slots_d, part_d)))
    zeros = (0, 0)
    block_c = pl.BlockSpec(part_c + (ff_rows, D), lambda t: at_c(t) + zeros)

    def call(name, kernel, ins, specs, outs, out_specs, megabytes, grid=None, scratch=()):
        many = isinstance(outs, tuple)
        if specs is None:
            specs = [SMEM if v is place or v is slot_mask else VMEM for v in ins]
            out_specs = (VMEM,) * (len(outs) if many else 1)
        elif not many:
            out_specs = (out_specs,)
        outs = outs if many else (outs,)
        body = kernel
        token = len(ins) + (links.last is not None) + len(outs)

        def kernel(*refs):
            return body(*refs[:token], *refs[token + 1 :])

        far = {(size, FF)} if name not in PINNED else {(size, FF)} | PINNED[name](size)
        outs = tuple(pltpu.HBM(o.shape, o.dtype) if o.shape in far else o for o in outs)
        streamed = lambda v: v.shape in far or (v.ndim > 2 and name in ("up", "slope", "middle", "down"))
        ins = tuple(pinned(v) if streamed(v) else v for v in ins)
        if grid is not None:
            compiler = params(megabytes)
        else:
            compiler = pltpu.CompilerParams(vmem_limit_bytes=megabytes << 20)

        def launch(last):
            return pl.pallas_call(
                kernel,
                out_shape=outs + (TOKEN,),
                in_specs=list(specs) + ([] if last is None else [ANY]),
                out_specs=tuple(out_specs) + (ANY,),
                scratch_shapes=list(scratch),
                compiler_params=compiler,
                cost_estimate=cost(links.length()),
                name=name,
                **({} if grid is None else {"grid": grid}),
            )(*ins, *([] if last is None else [pinned(last)]))

        out = links.run(launch)
        return out if many else out[0]

    def joined(*parts):
        arrays = tuple(part[0] for part in parts)
        ranges = tuple((first, last) for _, first, last in parts)
        width = sum(last - first for first, last in ranges)
        out = shape((1, arrays[0].shape[0], width), BF16)
        return call("join", functools.partial(join_kernel, ranges), arrays, None, out, None, 8)

    split = FIRST * tile
    vectors = (gain_first, shift_first, query_bias, value_bias, out_bias, gain_second, shift_second, down_bias, up_bias)
    wide_a = 3 * D + 128
    gather_b = joined((out_weight, 0, D), (up_weight, 0, split))
    gather_e = joined((up_weight, split, FF))
    x, dm = call(
        "spread",
        functools.partial(spread_kernel, images),
        (slot_mask, block_in, cotangent),
        None,
        (shape((size, D), BF16), shape((size, D), BF16)),
        None,
        16,
    )
    gather_a = call("line_up", line_up_kernel, (packed_weight,) + vectors, None, shape((1, rows, wide_a), BF16), None, 60)
    gather_c = down_weight[None]
    gather_c = links.advance(gather_c, hops["c"][0])
    gather_e = links.advance(gather_e, hops["e"][0])
    gather_b = links.advance(gather_b, hops["b"][0])
    gather_a = links.advance(gather_a, hops["a"][0])
    gather_c = links.advance(gather_c, hops["c"][1])
    gather_b = links.advance(gather_b, hops["b"][1])
    gather_e = links.advance(gather_e, hops["e"][1])
    gather_a = links.advance(gather_a, hops["a"][1])
    gather_c = links.advance(gather_c, hops["c"][2])
    gather_a = links.advance(gather_a, hops["a"][2])
    gather_e = links.advance(gather_e, hops["e"][2])
    gather_a = links.advance(gather_a, hops["a"][3])
    held_a, other_a = gather_a, links.swap(gather_a, 1, 1)
    gather_b = links.advance(gather_b, hops["b"][2])
    gather_e = links.advance(gather_e, hops["e"][3])
    held_e, other_e = gather_e, links.swap(gather_e, 1, 1)
    normed, qkv, attended, lse, vec = call(
        "attend",
        functools.partial(attend_kernel, flat["a"], rows),
        (place, x, held_a, other_a),
        None,
        (
            shape((size, D), BF16),
            shape((size, 3 * D), BF16),
            shape((size, D), BF16),
            shape((size, 128), F32),
            shape((16, D), F32),
        ),
        None,
        20,
        scratch=[pltpu.VMEM((D, 3 * D), BF16), pltpu.VMEM((D, 128), BF16)],
    )
    ubias = vec[8 : 8 + wide].reshape(wide, count, rows).transpose(1, 0, 2).reshape(1, FF)
    gather_b = links.advance(gather_b, hops["b"][3])
    held_b, other_b = gather_b, links.swap(gather_b, 1, 1)
    gather_c = links.advance(gather_c, hops["c"][3])
    held_c, other_c = gather_c.reshape(view_c + (ff_rows, D)), links.swap(gather_c, 1, 1).reshape(view_c + (ff_rows, D))
    block_b = pl.BlockSpec((number, rows, D), lambda t: (0, 0, jnp.minimum(t, FIRST)))
    block_e = pl.BlockSpec((number, rows, D), lambda t: (0, 0, jnp.maximum(t - FIRST - 1, 0)))
    dealt = pl.BlockSpec(part_d + (ff_rows, D), lambda t: at_d(before(t)) + zeros)
    middle, normed_two, active, slope, kept_d, sent_d = call(
        "up",
        functools.partial(up_kernel, flat["b"], flat["e"], slots_d, rows, ff_rows),
        (place, x, attended, dm, held_b, other_b, held_e, other_e, vec, ubias),
        [SMEM] + [fixed(size, D)] * 3 + [block_b, block_b, block_e, block_e, fixed(16, D), tiled(1, before)],
        (
            shape((size, D), F32),
            shape((size, D), BF16),
            shape((size, FF), BF16),
            shape((size, FF), F32),
            shape(view_d + (ff_rows, D), BF16),
            shape(view_d + (ff_rows, D), BF16),
        ),
        (fixed(size, D), fixed(size, D), tiled(size, before), tiled(size, before), dealt, dealt),
        30,
        grid=(depth + 1,),
        scratch=[pltpu.VMEM((D, D), BF16)],
    )
    parts_d = links.exchange(kept_d, sent_d)
    block_u = pl.BlockSpec((number, rows, D), lambda t: (0, 0, t))
    low, kept_u, sent_u, usums = call(
        "slope",
        functools.partial(slope_kernel, flat["u"], slots_c, rows, ff_rows),
        (place, dm, normed_two, slope, held_c, other_c),
        [SMEM, fixed(size, D), fixed(size, D), tiled(size, same), block_c, block_c],
        (shape((size, FF), BF16), pieces(FF), pieces(FF), shape((D, 128), F32)),
        (tiled(size, same), block_u, block_u, pl.BlockSpec((D // depth, 128), lambda t: (t, 0))),
        22,
        grid=(depth,),
        scratch=[pltpu.VMEM((D, D), BF16)],
    )
    parts_u = links.exchange(kept_u, sent_u)
    parts_d = links.reduce(parts_d, hops["d"][0])
    block_b = pl.BlockSpec((number, rows, D), lambda t: (0, 0, jnp.where(t == depth, 0, jnp.minimum(t + 1, FIRST))))
    block_e = pl.BlockSpec((number, rows, D), lambda t: (0, 0, jnp.clip(t - FIRST, 0, depth - FIRST - 1)))
    datt, dmid, kept_o, sent_o, sums = call(
        "middle",
        functools.partial(middle_kernel, flat["b"], flat["e"], flat["i"], rows),
        (place, low, middle, dm, attended, held_b, other_b, held_e, other_e, vec),
        [SMEM, tiled(size, upto)] + [fixed(size, D)] * 3 + [block_b, block_b, block_e, block_e, fixed(16, D)],
        (shape((size, D), BF16), shape((size, D), F32), pieces(D), pieces(D), shape((8, D), F32)),
        (fixed(size, D), fixed(size, D), whole(D), whole(D), fixed(8, D)),
        26,
        grid=(depth + 1,),
        scratch=[pltpu.VMEM((D, D), BF16), pltpu.VMEM((size, D), F32)],
    )
    parts_u = links.reduce(parts_u, hops["u"][0])
    def heads(group, first, beside, *more):
        cols = beside + 3 * D // 2
        return call(
            "heads",
            functools.partial(heads_kernel, flat[group], rows, first, beside),
            (place, qkv, datt, lse, normed) + more,
            None,
            (shape((size, 3 * D // 2), BF16), pieces(cols), pieces(cols)),
            None,
            16,
        )

    half_a, kept_i, sent_i = heads("i", 0, D, kept_o, sent_o)
    parts_i = links.exchange(kept_i, sent_i)
    parts_d = links.reduce(parts_d, hops["d"][1])
    half_b, kept_h, sent_h = heads("j", HEADS // 4, 0)
    parts_u = links.reduce(parts_u, hops["u"][1])
    parts_i = links.reduce(parts_i, hops["i"][0])
    wide_j = 3 * D // 2 + 128
    kept_j, sent_j, igrad = call(
        "inward",
        functools.partial(input_kernel, flat["a"], flat["j"], rows),
        (place, x, dmid, half_a, half_b, kept_h, sent_h, held_a, other_a, vec, sums, usums),
        None,
        (pieces(wide_j), pieces(wide_j), shape((tokens, D), F32)),
        None,
        22,
        scratch=[pltpu.VMEM((D, 3 * D), BF16)],
    )
    parts_j = links.exchange(kept_j, sent_j)
    parts_d = links.reduce(parts_d, hops["d"][2])
    parts_j = links.reduce(parts_j, hops["j"][0])
    parts_u = links.reduce(parts_u, hops["u"][2])
    parts_i = links.reduce(parts_i, hops["i"][1])
    parts_d = links.reduce(parts_d, hops["d"][3])
    parts_j = links.reduce(parts_j, hops["j"][1])
    parts_i = links.reduce(parts_i, hops["i"][2])
    parts_j = links.reduce(parts_j, hops["j"][2])
    parts_u = links.reduce(parts_u, hops["u"][3])
    block_out = call(
        "down",
        functools.partial(down_kernel, slots_c, ff_rows),
        (place, slot_mask, active, middle, held_c, other_c, vec),
        [SMEM, SMEM, tiled(size, same), fixed(size, D), block_c, block_c, fixed(16, D)],
        shape((tokens, D), BF16),
        fixed(tokens, D),
        18,
        grid=(depth,),
        scratch=[pltpu.VMEM((D, D), BF16), pltpu.VMEM((size, D), F32)],
    )
    parts_i = links.reduce(parts_i, hops["i"][3])
    parts_j = links.reduce(parts_j, hops["j"][3])
    grads_d, grads_u, grads_i, grads_j = (settle(parts) for parts in (parts_d, parts_u, parts_i, parts_j))
    half = D // 2
    grads_packed = []
    for part in range(3):
        grads_packed += [grads_i[:, D + part * half : D + (part + 1) * half], grads_j[:, part * half : (part + 1) * half]]
    small = grads_j[:, 3 * half : 3 * half + 8 + wide].T
    return (
        block_out,
        igrad,
        small[0],
        small[1],
        jnp.concatenate(grads_packed, axis=1),
        small[2],
        small[3],
        grads_i[:, :D],
        small[4],
        small[5],
        small[6],
        grads_u,
        small[8:].reshape(-1),
        grads_d,
        small[7],
    )


def solution(mesh):
    row, flat = P("dp", None), P("dp")
    in_specs = (row, flat, flat, flat, row, flat, flat, row, flat, flat, flat, row, flat, row, flat, row)
    out_specs = (row, row, flat, flat, row, flat, flat, row, flat, flat, flat, row, flat, row, flat)
    return jax.shard_map(shards, mesh=mesh, in_specs=in_specs, out_specs=out_specs, check_vma=False)
```

```python
import functools

import jax
import jax.numpy as jnp
from jax import lax
from jax.experimental import pallas as pl
from jax.experimental.pallas import tpu as pltpu
from jax.sharding import PartitionSpec as P

D = 768
HEADS = 12
HEAD_DIM = 64
FF = 3072
LEN = 197
SLOT = 208
SPEED = 1.15e9
LENGTHS = (1, 8, 0.25, 0.5, 24, 1, 1, 24, 0.25, 1, 2, 0.25, 1, 8, 3, 24, 1, 0.25, 0.25, 8, 2, 6, 0.25, 12, 1, 2, 1, 16, 2, 1, 32, 2, 32, 0.25, 4, 0.5, 0.25, 0.5, 6, 24, 0.5, 2, 1, 8)
ORDERS = {'a': 'fnxx', 'b': 'fxnx', 'e': 'xfxn', 'c': 'nxfx', 'd': 'xnfx', 'u': 'xnxf', 'i': 'xxfn', 'j': 'xxnf'}
GATHERS = ("a", "b", "e", "c")
FIRST = 2
PINNED = {}
SCALE = HEAD_DIM ** (-0.5)
F32 = jnp.float32
BF16 = jnp.bfloat16
VMEM = pl.BlockSpec(memory_space=pltpu.VMEM)
SMEM = pl.BlockSpec(memory_space=pltpu.SMEM)
ANY = pl.BlockSpec(memory_space=pl.ANY)
TOKEN = pltpu.HBM((8, 128), F32)


def params(megabytes):
    return pltpu.CompilerParams(
        vmem_limit_bytes=megabytes << 20, dimension_semantics=("arbitrary",)
    )


def cost(length):
    return pl.CostEstimate(flops=int(length * SPEED), transcendentals=0, bytes_accessed=D)


def mul(a, b):
    return jnp.dot(a, b, preferred_element_type=F32)


def mul_t(a, b):
    return lax.dot_general(a, b, (((1,), (1,)), ((), ())), preferred_element_type=F32)


def t_mul(a, b):
    return lax.dot_general(a, b, (((0,), (0,)), ((), ())), preferred_element_type=F32)


class Links:
    def __init__(self, count):
        chips = count // 2
        z = min(4, chips)
        plane = chips // z
        x = 1
        while x * x < plane:
            x *= 2
        self.count, self.z, self.plane = count, z, plane
        bit = 2
        x_bits, y_bits, z_bits = [], [], []
        for bits, extent in ((x_bits, x), (y_bits, plane // x), (z_bits, z)):
            size = 1
            while size < extent:
                bits.append(bit)
                bit *= 2
                size *= 2
        across = list(zip(x_bits + y_bits, y_bits + x_bits))
        half = (len(across) + 1) // 2
        self.near = [(b, b) for b in z_bits[:1]]
        self.far = [(b, b) for b in z_bits[1:]]
        self.across = across[:half], across[half:]
        self.all = self.near + self.far + across
        index = lax.axis_index("dp")
        core = index % 2
        sides = [((index & jnp.where(core == 0, *step)) != 0).astype(jnp.int32) for step in self.all]
        self.place = jnp.stack([core.astype(jnp.int32)] + sides)
        self.last = None
        self.lengths = iter(LENGTHS + (1,) * 64)

    def length(self):
        return next(self.lengths)

    def hops(self, order):
        found, crossed = [], 0
        for kind in order:
            if kind == "x":
                found.append(self.across[crossed])
                crossed += 1
            else:
                found.append(self.far if kind == "f" else self.near)
        return found

    def steps(self, order, scatter):
        steps = [step for hop in self.hops(order) for step in hop]
        return steps[::-1] if scatter else steps

    def slots(self, order, scatter):
        steps = self.steps(order, scatter)
        found = []
        for device in range(self.count):
            bits = [1 if device & step[device % 2] else 0 for step in steps]
            found.append((device % 2, sum(b << weight for weight, b in enumerate(bits))))
        return tuple(found)

    def tiles(self, order, scatter):
        steps = self.steps(order, scatter)[::-1]
        along = [step in self.near or step in self.far for step in steps]
        block = tuple(1 if z else 2 for z in along)

        def index(t):
            return tuple((t % 2 if step in self.near else t // 2) if z else 0 for step, z in zip(steps, along))

        found = []
        for device in range(self.count // self.z):
            found.append((device % 2, tuple(1 if device & step[device % 2] else 0 for step in steps)))
        return (2,) * len(steps), block, index, tuple(found)

    def run(self, kernel, *args, **options):
        *out, self.last = kernel(self.last, *args, **options)
        return tuple(out)

    def swap(self, value, even, odd):
        pairs = [(i, i ^ (odd if i % 2 else even)) for i in range(self.count)]
        return lax.ppermute(value, "dp", pairs)

    def pair(self, step, held, other):
        count, rows, width = held.shape
        at = self.all.index(step)

        def body(place, held, other, *refs):
            out = refs[-2]
            high = place[1 + at]

            def copy(i, carry):
                out[high, i] = held[i]
                out[1 - high, i] = other[i]
                return carry

            lax.fori_loop(0, count, copy, 0)

        def kernel(last):
            return pl.pallas_call(
                body,
                out_shape=(jax.ShapeDtypeStruct((2, count, rows, width), BF16), TOKEN),
                in_specs=[SMEM, VMEM, VMEM] + ([] if last is None else [ANY]),
                out_specs=(VMEM, ANY),
                compiler_params=pltpu.CompilerParams(vmem_limit_bytes=10 << 20),
                cost_estimate=cost(self.length()),
                name="pair",
            )(self.place, held, other, *([] if last is None else [pinned(last)]))

        return self.run(kernel)[0].reshape(2 * count, rows, width)

    def advance(self, held, hop):
        for step in hop:
            held = self.pair(step, held, self.swap(held, *step))
        return held

    def exchange(self, kept, sent):
        other = self.swap(sent, 1, 1)
        shape = (-1,) + kept.shape[-2:]
        return kept.reshape(shape), other.reshape(shape)

    def halve(self, step, kept, other):
        at = self.all.index(step)
        half = kept.shape[0] // 2
        chunk = max(1, half // 4)
        grid = half // chunk
        block = (chunk,) + kept.shape[1:]
        upper = pl.BlockSpec(block, lambda i, place: (place[1 + at] * grid + i, 0, 0))
        lower = pl.BlockSpec(block, lambda i, place: ((1 - place[1 + at]) * grid + i, 0, 0))
        straight = pl.BlockSpec(block, lambda i, place: (i, 0, 0))

        def body(place, kept_up, kept_low, other_up, other_low, last, stay, leave, token):
            stay[...] = kept_up[...].astype(F32) + other_up[...].astype(F32)
            leave[...] = (kept_low[...].astype(F32) + other_low[...].astype(F32)).astype(BF16)

        def kernel(last):
            return pl.pallas_call(
                body,
                grid_spec=pltpu.PrefetchScalarGridSpec(
                    num_scalar_prefetch=1,
                    grid=(grid,),
                    in_specs=[upper, lower, upper, lower, ANY],
                    out_specs=(straight, straight, ANY),
                ),
                out_shape=(
                    jax.ShapeDtypeStruct((half,) + kept.shape[1:], F32),
                    jax.ShapeDtypeStruct((half,) + kept.shape[1:], BF16),
                    TOKEN,
                ),
                compiler_params=params(12),
                cost_estimate=cost(self.length()),
                name="halve",
            )(self.place, kept, kept, other, other, pinned(last))

        return self.run(kernel)

    def reduce(self, parts, hop):
        for step in hop:
            kept, low = self.halve(step, *parts)
            parts = kept, self.swap(low, *step)
        return parts


def pinned(value):
    return pltpu.with_memory_space_constraint(value, pltpu.HBM)


def settle(parts):
    return parts[0][0].astype(F32) + parts[1][0].astype(F32)


def collect(into, rows, slots, core, held, other, cols=slice(None)):
    @pl.when(core == 0)
    def _():
        for place, (parity, piece) in enumerate(slots):
            source = other if parity else held
            into[place * rows : (place + 1) * rows, :] = source[piece + (slice(None), cols)]

    @pl.when(core == 1)
    def _():
        for place, (parity, piece) in enumerate(slots):
            source = held if parity else other
            into[place * rows : (place + 1) * rows, :] = source[piece + (slice(None), cols)]


def deal(values, rows, slots, core, kept, sent, cols=slice(None)):
    halves = ({}, {})
    for place, (parity, piece) in enumerate(slots):
        halves[parity][piece] = values[place * rows : (place + 1) * rows, :]
    for piece, even in halves[0].items():
        odd = halves[1][piece]
        kept[piece + (slice(None), cols)] = jnp.where(core == 0, even, odd)
        sent[piece + (slice(None), cols)] = jnp.where(core == 0, odd, even)


def standard(values):
    centred = values - jnp.mean(values, axis=-1, keepdims=True)
    rate = lax.rsqrt(jnp.mean(centred * centred, axis=-1, keepdims=True) + 1e-06)
    return centred * rate, rate


def standard_back(grad, gain, standardised, rate):
    pushed = grad * gain
    along = jnp.mean(pushed * standardised, axis=-1, keepdims=True)
    inner = pushed - jnp.mean(pushed, axis=-1, keepdims=True) - standardised * along
    sums = (jnp.sum(grad * standardised, axis=0, keepdims=True), jnp.sum(grad, axis=0, keepdims=True))
    return (rate * inner,) + sums


def first_half(width):
    return lax.broadcasted_iota(jnp.int32, (SLOT, 2 * HEAD_DIM), 1) < HEAD_DIM


def line_up_kernel(weight, *refs):
    lines, bias, out = refs[:8], refs[8], refs[-1]
    rows = weight.shape[0]
    out[0, :, : 3 * D] = weight[...]
    lines = [line[...].astype(F32).reshape(1, rows) for line in lines]
    bias = bias[...].astype(F32).reshape(1, -1)
    lines += [bias[:, at : at + rows] for at in range(0, bias.shape[1], rows)]
    lines.append(jnp.zeros((128 - len(lines), rows), F32))
    out[0, :, 3 * D :] = jnp.concatenate(lines, axis=0).T.astype(BF16)


def spread_kernel(images, live, block_in, cotangent, earlier, x_ref, dm_ref):
    for ref, into in ((block_in, x_ref), (cotangent, dm_ref)):
        values = ref[...].astype(F32)
        for image in range(images):
            part = values[image * LEN : (image + 1) * LEN]
            if into is dm_ref:
                part = jnp.where(live[image * LEN] != 0, part, 0.0)
            part = jnp.concatenate([part, jnp.zeros((SLOT - LEN, D), F32)], axis=0)
            into[image * SLOT : (image + 1) * SLOT, :] = part.astype(BF16)


def trim(values):
    parts = [values[at : at + LEN] for at in range(0, values.shape[0], SLOT)]
    return jnp.concatenate(parts, axis=0)


def join_kernel(ranges, *refs):
    out = refs[-1]
    start = 0
    for part, (first, last) in zip(refs, ranges):
        out[0, :, start : start + last - first] = part[:, first:last]
        start += last - first


def attend_kernel(slots, rows, place, x_ref, held, other, earlier, normed, qkv, attended, lse, vec, weight, columns):
    core = place[0]
    collect(weight, rows, slots, core, held, other, slice(0, 3 * D))
    collect(columns, rows, slots, core, held, other, slice(3 * D, 3 * D + 128))
    vec[...] = columns[...].astype(F32).T[: vec.shape[0], :]
    shaped, _ = standard(x_ref[...].astype(F32))
    low = (shaped * vec[0:1, :] + vec[1:2, :]).astype(BF16)
    normed[...] = low
    for part, row in ((0, 2), (1, None), (2, 3)):
        cols = pl.ds(part * D, D)
        packed = mul(low, weight[:, cols])
        if row is not None:
            packed = packed + vec[row : row + 1, :]
        qkv[:, cols] = packed.astype(BF16)
    left = first_half(0)
    real = lax.broadcasted_iota(jnp.int32, (SLOT, SLOT), 1) < LEN
    lane = lax.broadcasted_iota(jnp.int32, (SLOT, 128), 1)
    images = x_ref.shape[0] // SLOT
    lse[...] = jnp.zeros_like(lse)

    def pair_step(at, carry):
        image, pair = at // (HEADS // 2), at % (HEADS // 2)
        tokens = pl.ds(pl.multiple_of(image * SLOT, 16), SLOT)
        cols = lambda part: pl.ds(pl.multiple_of(part * D + pair * 128, 128), 128)
        query, key, value = qkv[tokens, cols(0)], qkv[tokens, cols(1)], qkv[tokens, cols(2)]
        mixed, logs = [], lse[tokens, :]
        for side in range(2):
            chosen = left if side == 0 else ~left
            scores = mul_t(jnp.where(chosen, query, jnp.zeros_like(query)), key) * SCALE
            scores = jnp.where(real, scores, -1e30)
            top = jnp.max(scores, axis=-1, keepdims=True)
            raised = jnp.exp(scores - top)
            total = jnp.sum(raised, axis=-1, keepdims=True)
            logs = jnp.where(lane == pair * 2 + side, top + jnp.log(total), logs)
            mixed.append(mul((raised * (1.0 / total)).astype(BF16), value))
        lse[tokens, :] = logs
        attended[tokens, cols(0)] = jnp.where(left, mixed[0], mixed[1]).astype(BF16)
        return carry

    lax.fori_loop(0, images * (HEADS // 2), pair_step, 0, unroll=HEADS // 2)


def up_kernel(slots_b, slots_e, slots_d, rows, ff_rows, place, x_ref, attended, dm, held, other, held_e, other_e, vec, ubias, earlier, middle, normed, active, slope, kept, sent, weight):
    core = place[0]
    step = pl.program_id(0)

    @pl.when(step <= FIRST)
    def _():
        collect(weight, rows, slots_b, core, held, other)

    @pl.when(step > FIRST)
    def _():
        collect(weight, rows, slots_e, core, held_e, other_e)

    @pl.when(step == 0)
    def _():
        total = x_ref[...].astype(F32) + mul(attended[...], weight[...]) + vec[4:5, :]
        middle[...] = total
        shaped, _ = standard(total)
        normed[...] = (shaped * vec[5:6, :] + vec[6:7, :]).astype(BF16)

    @pl.when(step > 0)
    def _():
        pre = mul(normed[...], weight[...]) + ubias[0:1, :]
        share = 0.5 + 0.5 * lax.erf(pre * (0.5**0.5))
        low = (pre * share).astype(BF16)
        active[...] = low
        slope[...] = share + pre * (jnp.exp(pre * pre * -0.5) * 0.3989422804014327)
        grad = t_mul(low, dm[...]).astype(BF16)

        deal(grad, ff_rows, slots_d, core, kept, sent)


def slope_kernel(slots_u, slots_c, rows, ff_rows, place, dm, normed, slope, held, other, earlier, low, kept, sent, sums, weight):
    core = place[0]
    collect(weight, ff_rows, slots_c, core, held, other)
    grad = (mul_t(dm[...], weight[...]) * slope[...]).astype(BF16)
    low[...] = grad
    deal(t_mul(normed[...], grad).astype(BF16), rows, slots_u, core, kept, sent)
    lines = jnp.broadcast_to(jnp.sum(grad.astype(F32), axis=0, keepdims=True), (128, grad.shape[1])).T
    lane = lax.broadcasted_iota(jnp.int32, (rows, 128), 1)
    for device in range(grad.shape[1] // ff_rows):
        total = jnp.zeros((rows, 128), F32)
        for at in range(ff_rows // rows):
            start = device * ff_rows + at * rows
            total = jnp.where(lane == 8 + at, lines[start : start + rows, :], total)
        sums[device * rows : (device + 1) * rows, :] = total


def middle_kernel(slots_b, slots_e, slots_i, rows, place, low, middle, dm, attended, held, other, held_e, other_e, vec, earlier, datt, dmid, kept, sent, sums, weight, back):
    core = place[0]
    step = pl.program_id(0)
    last = pl.num_programs(0) - 1

    @pl.when((step < FIRST) | (step == last))
    def _():
        collect(weight, rows, slots_b, core, held, other)

    @pl.when((step >= FIRST) & (step < last))
    def _():
        collect(weight, rows, slots_e, core, held_e, other_e)

    @pl.when(step == 0)
    def _():
        back[...] = mul_t(low[...], weight[...])

    @pl.when((step > 0) & (step < last))
    def _():
        back[...] += mul_t(low[...], weight[...])

    @pl.when(step == last)
    def _():
        source = dm[...].astype(F32)
        shaped, rate = standard(middle[...])
        inner, ggain, gshift = standard_back(back[...], vec[5:6, :], shaped, rate)
        total = source + inner
        dmid[...] = total
        branch = total.astype(BF16)
        datt[...] = mul_t(branch, weight[...]).astype(BF16)
        deal(t_mul(attended[...], branch).astype(BF16), rows, slots_i, core, kept, sent)
        gout = jnp.sum(branch.astype(F32), axis=0, keepdims=True)
        gdown = jnp.sum(source, axis=0, keepdims=True)
        sums[...] = jnp.concatenate([gout, ggain, gshift, gdown] * 2, axis=0)


def down_kernel(slots_c, ff_rows, place, live, active, middle, held, other, vec, earlier, result, weight, mixed):
    core = place[0]
    step = pl.program_id(0)
    collect(weight, ff_rows, slots_c, core, held, other)
    more = mul(active[...], weight[...])

    @pl.when(step == 0)
    def _():
        mixed[...] = more

    @pl.when(step > 0)
    def _():
        mixed[...] += more

    @pl.when(step == pl.num_programs(0) - 1)
    def _():
        full = middle[...] + mixed[...] + vec[7:8, :]
        images = full.shape[0] // SLOT
        keep = [jnp.where(live[i * LEN] != 0, full[i * SLOT : i * SLOT + LEN], 0.0) for i in range(images)]
        result[...] = jnp.concatenate(keep, axis=0).astype(BF16)


def heads_kernel(slots, rows, first, beside, place, qkv, datt, lse, normed, *refs):
    more, (earlier, dqkv, kept, sent) = refs[:-4], refs[-4:]
    core = place[0]
    left = first_half(0)
    real = lax.broadcasted_iota(jnp.int32, (SLOT, SLOT), 1) < LEN
    lane = lax.broadcasted_iota(jnp.int32, (SLOT, 128), 1)
    pairs = HEADS // 4
    images = qkv.shape[0] // SLOT
    for source, into in zip(more, (kept, sent)):
        into[:, :, :beside] = source[...]

    def pair_step(at, carry):
        image, local = at // pairs, at % pairs
        pair = first + local
        tokens = pl.ds(pl.multiple_of(image * SLOT, 16), SLOT)
        cols = lambda part: pl.ds(pl.multiple_of(part * D + pair * 128, 128), 128)
        query, key, value = qkv[tokens, cols(0)], qkv[tokens, cols(1)], qkv[tokens, cols(2)]
        grad, logs = datt[tokens, cols(0)], lse[tokens, :]
        dq, dk, dv = [], [], []
        for side in range(2):
            chosen = left if side == 0 else ~left
            scores = mul_t(jnp.where(chosen, query, jnp.zeros_like(query)), key) * SCALE
            log = jnp.sum(jnp.where(lane == pair * 2 + side, logs, 0.0), axis=-1, keepdims=True)
            attn = jnp.where(real, jnp.exp(scores - log), 0.0)
            dattn = mul_t(jnp.where(chosen, grad, jnp.zeros_like(grad)), value)
            dscores = (attn * (dattn - jnp.sum(attn * dattn, axis=-1, keepdims=True))).astype(BF16)
            dv.append(t_mul(attn.astype(BF16), grad))
            dq.append(mul(dscores, key) * SCALE)
            dk.append(t_mul(dscores, query) * SCALE)
        for part, halves in ((0, dq), (1, dk), (2, dv)):
            into = pl.ds(pl.multiple_of(part * (D // 2) + local * 128, 128), 128)
            dqkv[tokens, into] = jnp.where(left, halves[0], halves[1]).astype(BF16)
        return carry

    lax.fori_loop(0, images * pairs, pair_step, 0, unroll=images * pairs)
    grad = t_mul(normed[...], dqkv[...]).astype(BF16)
    deal(grad, rows, slots, core, kept, sent, slice(beside, beside + 3 * D // 2))


def input_kernel(slots_a, slots_j, rows, place, x_ref, dmid, half_a, half_b, kept_b, sent_b, held, other, vec, sums, usums, earlier, kept, sent, igrad, weight):
    core = place[0]
    for source, into in ((kept_b, kept), (sent_b, sent)):
        into[:, :, : source.shape[2]] = source[...]
    collect(weight, rows, slots_a, core, held, other, slice(0, 3 * D))
    back = None
    rowsums = []
    for part in range(3):
        cols = pl.ds(part * (D // 2), D // 2)
        low = jnp.concatenate([half_a[:, cols], half_b[:, cols]], axis=1)
        rowsums.append(jnp.sum(low.astype(F32), axis=0, keepdims=True))
        more = mul_t(low, weight[:, pl.ds(part * D, D)])
        back = more if back is None else back + more
    shaped, rate = standard(x_ref[...].astype(F32))
    inner, ggain, gshift = standard_back(back, vec[0:1, :], shaped, rate)
    igrad[...] = trim(dmid[...] + inner)
    lines = [ggain, gshift, rowsums[0], rowsums[2], sums[0:4, :]]
    lines.append(jnp.zeros((128 - 8, D), F32))
    columns = (jnp.concatenate(lines, axis=0).T + usums[...]).astype(BF16)
    deal(columns, rows, slots_j, core, kept, sent, slice(kept_b.shape[2], kept_b.shape[2] + 128))


def zeroed(piece, part):
    return tuple(0 if extent == 1 else bit for bit, extent in zip(piece, part))


def shards(
    block_in,
    slot_mask,
    gain_first,
    shift_first,
    packed_weight,
    query_bias,
    value_bias,
    out_weight,
    out_bias,
    gain_second,
    shift_second,
    up_weight,
    up_bias,
    down_weight,
    down_bias,
    cotangent,
):
    links = Links(lax.axis_size("dp"))
    rows = packed_weight.shape[0]
    ff_rows = down_weight.shape[0]
    wide = ff_rows // rows
    count, depth = links.count, links.z
    number = count // 2
    place = links.place
    tokens = block_in.shape[0]
    images = tokens // LEN
    size = images * SLOT
    hops = {group: links.hops(order) for group, order in ORDERS.items()}
    slots = {group: links.slots(order, group not in GATHERS) for group, order in ORDERS.items()}
    flat = {group: tuple((parity, (piece,)) for parity, piece in found) for group, found in slots.items()}
    shape = jax.ShapeDtypeStruct
    pieces = lambda cols: shape((number, rows, cols), BF16)
    fixed = lambda height, width: pl.BlockSpec((height, width), lambda t: (0, 0))
    tile = FF // depth
    tiled = lambda height, at: pl.BlockSpec((height, tile), lambda t: (0, at(t)))
    whole = lambda cols: pl.BlockSpec((number, rows, cols), lambda t: (0, 0, 0))
    before = lambda t: jnp.maximum(t - 1, 0)
    upto = lambda t: jnp.minimum(t, depth - 1)
    same = lambda t: t
    view_c, part_c, at_c, slots_c = links.tiles(ORDERS["c"], False)
    view_d, part_d, at_d, slots_d = links.tiles(ORDERS["d"], True)
    slots_c, slots_d = (tuple((parity, zeroed(piece, part)) for parity, piece in found) for found, part in ((slots_c, part_c), (slots_d, part_d)))
    zeros = (0, 0)
    block_c = pl.BlockSpec(part_c + (ff_rows, D), lambda t: at_c(t) + zeros)

    def call(name, kernel, ins, specs, outs, out_specs, megabytes, grid=None, scratch=()):
        many = isinstance(outs, tuple)
        if specs is None:
            specs = [SMEM if v is place or v is slot_mask else VMEM for v in ins]
            out_specs = (VMEM,) * (len(outs) if many else 1)
        elif not many:
            out_specs = (out_specs,)
        outs = outs if many else (outs,)
        body = kernel
        token = len(ins) + (links.last is not None) + len(outs)

        def kernel(*refs):
            return body(*refs[:token], *refs[token + 1 :])

        far = {(size, FF)} if name not in PINNED else {(size, FF)} | PINNED[name](size)
        outs = tuple(pltpu.HBM(o.shape, o.dtype) if o.shape in far else o for o in outs)
        streamed = lambda v: v.shape in far or (v.ndim > 2 and name in ("up", "slope", "middle", "down"))
        ins = tuple(pinned(v) if streamed(v) else v for v in ins)
        if grid is not None:
            compiler = params(megabytes)
        else:
            compiler = pltpu.CompilerParams(vmem_limit_bytes=megabytes << 20)

        def launch(last):
            return pl.pallas_call(
                kernel,
                out_shape=outs + (TOKEN,),
                in_specs=list(specs) + ([] if last is None else [ANY]),
                out_specs=tuple(out_specs) + (ANY,),
                scratch_shapes=list(scratch),
                compiler_params=compiler,
                cost_estimate=cost(links.length()),
                name=name,
                **({} if grid is None else {"grid": grid}),
            )(*ins, *([] if last is None else [pinned(last)]))

        out = links.run(launch)
        return out if many else out[0]

    def joined(*parts):
        arrays = tuple(part[0] for part in parts)
        ranges = tuple((first, last) for _, first, last in parts)
        width = sum(last - first for first, last in ranges)
        out = shape((1, arrays[0].shape[0], width), BF16)
        return call("join", functools.partial(join_kernel, ranges), arrays, None, out, None, 8)

    split = FIRST * tile
    vectors = (gain_first, shift_first, query_bias, value_bias, out_bias, gain_second, shift_second, down_bias, up_bias)
    wide_a = 3 * D + 128
    gather_a = call("line_up", line_up_kernel, (packed_weight,) + vectors, None, shape((1, rows, wide_a), BF16), None, 60)
    gather_e = joined((up_weight, split, FF))
    gather_b = joined((out_weight, 0, D), (up_weight, 0, split))
    gather_a = links.advance(gather_a, hops["a"][0])
    gather_c = down_weight[None]
    gather_c = links.advance(gather_c, hops["c"][0])
    gather_b = links.advance(gather_b, hops["b"][0])
    gather_e = links.advance(gather_e, hops["e"][0])
    gather_a = links.advance(gather_a, hops["a"][1])
    gather_b = links.advance(gather_b, hops["b"][1])
    x, dm = call(
        "spread",
        functools.partial(spread_kernel, images),
        (slot_mask, block_in, cotangent),
        None,
        (shape((size, D), BF16), shape((size, D), BF16)),
        None,
        16,
    )
    gather_c = links.advance(gather_c, hops["c"][1])
    gather_a = links.advance(gather_a, hops["a"][2])
    gather_e = links.advance(gather_e, hops["e"][1])
    gather_b = links.advance(gather_b, hops["b"][2])
    gather_a = links.advance(gather_a, hops["a"][3])
    held_a, other_a = gather_a, links.swap(gather_a, 1, 1)
    gather_e = links.advance(gather_e, hops["e"][2])
    gather_c = links.advance(gather_c, hops["c"][2])
    normed, qkv, attended, lse, vec = call(
        "attend",
        functools.partial(attend_kernel, flat["a"], rows),
        (place, x, held_a, other_a),
        None,
        (
            shape((size, D), BF16),
            shape((size, 3 * D), BF16),
            shape((size, D), BF16),
            shape((size, 128), F32),
            shape((16, D), F32),
        ),
        None,
        20,
        scratch=[pltpu.VMEM((D, 3 * D), BF16), pltpu.VMEM((D, 128), BF16)],
    )
    ubias = vec[8 : 8 + wide].reshape(wide, count, rows).transpose(1, 0, 2).reshape(1, FF)
    gather_b = links.advance(gather_b, hops["b"][3])
    held_b, other_b = gather_b, links.swap(gather_b, 1, 1)
    gather_e = links.advance(gather_e, hops["e"][3])
    held_e, other_e = gather_e, links.swap(gather_e, 1, 1)
    gather_c = links.advance(gather_c, hops["c"][3])
    held_c, other_c = gather_c.reshape(view_c + (ff_rows, D)), links.swap(gather_c, 1, 1).reshape(view_c + (ff_rows, D))
    block_b = pl.BlockSpec((number, rows, D), lambda t: (0, 0, jnp.minimum(t, FIRST)))
    block_e = pl.BlockSpec((number, rows, D), lambda t: (0, 0, jnp.maximum(t - FIRST - 1, 0)))
    dealt = pl.BlockSpec(part_d + (ff_rows, D), lambda t: at_d(before(t)) + zeros)
    middle, normed_two, active, slope, kept_d, sent_d = call(
        "up",
        functools.partial(up_kernel, flat["b"], flat["e"], slots_d, rows, ff_rows),
        (place, x, attended, dm, held_b, other_b, held_e, other_e, vec, ubias),
        [SMEM] + [fixed(size, D)] * 3 + [block_b, block_b, block_e, block_e, fixed(16, D), tiled(1, before)],
        (
            shape((size, D), F32),
            shape((size, D), BF16),
            shape((size, FF), BF16),
            shape((size, FF), F32),
            shape(view_d + (ff_rows, D), BF16),
            shape(view_d + (ff_rows, D), BF16),
        ),
        (fixed(size, D), fixed(size, D), tiled(size, before), tiled(size, before), dealt, dealt),
        30,
        grid=(depth + 1,),
        scratch=[pltpu.VMEM((D, D), BF16)],
    )
    parts_d = links.exchange(kept_d, sent_d)
    block_u = pl.BlockSpec((number, rows, D), lambda t: (0, 0, t))
    low, kept_u, sent_u, usums = call(
        "slope",
        functools.partial(slope_kernel, flat["u"], slots_c, rows, ff_rows),
        (place, dm, normed_two, slope, held_c, other_c),
        [SMEM, fixed(size, D), fixed(size, D), tiled(size, same), block_c, block_c],
        (shape((size, FF), BF16), pieces(FF), pieces(FF), shape((D, 128), F32)),
        (tiled(size, same), block_u, block_u, pl.BlockSpec((D // depth, 128), lambda t: (t, 0))),
        22,
        grid=(depth,),
        scratch=[pltpu.VMEM((D, D), BF16)],
    )
    parts_u = links.exchange(kept_u, sent_u)
    parts_d = links.reduce(parts_d, hops["d"][0])
    block_b = pl.BlockSpec((number, rows, D), lambda t: (0, 0, jnp.where(t == depth, 0, jnp.minimum(t + 1, FIRST))))
    block_e = pl.BlockSpec((number, rows, D), lambda t: (0, 0, jnp.clip(t - FIRST, 0, depth - FIRST - 1)))
    datt, dmid, kept_o, sent_o, sums = call(
        "middle",
        functools.partial(middle_kernel, flat["b"], flat["e"], flat["i"], rows),
        (place, low, middle, dm, attended, held_b, other_b, held_e, other_e, vec),
        [SMEM, tiled(size, upto)] + [fixed(size, D)] * 3 + [block_b, block_b, block_e, block_e, fixed(16, D)],
        (shape((size, D), BF16), shape((size, D), F32), pieces(D), pieces(D), shape((8, D), F32)),
        (fixed(size, D), fixed(size, D), whole(D), whole(D), fixed(8, D)),
        26,
        grid=(depth + 1,),
        scratch=[pltpu.VMEM((D, D), BF16), pltpu.VMEM((size, D), F32)],
    )
    parts_u = links.reduce(parts_u, hops["u"][0])
    def heads(group, first, beside, *more):
        cols = beside + 3 * D // 2
        return call(
            "heads",
            functools.partial(heads_kernel, flat[group], rows, first, beside),
            (place, qkv, datt, lse, normed) + more,
            None,
            (shape((size, 3 * D // 2), BF16), pieces(cols), pieces(cols)),
            None,
            16,
        )

    half_a, kept_i, sent_i = heads("i", 0, D, kept_o, sent_o)
    parts_i = links.exchange(kept_i, sent_i)
    parts_d = links.reduce(parts_d, hops["d"][1])
    half_b, kept_h, sent_h = heads("j", HEADS // 4, 0)
    parts_i = links.reduce(parts_i, hops["i"][0])
    parts_u = links.reduce(parts_u, hops["u"][1])
    wide_j = 3 * D // 2 + 128
    kept_j, sent_j, igrad = call(
        "inward",
        functools.partial(input_kernel, flat["a"], flat["j"], rows),
        (place, x, dmid, half_a, half_b, kept_h, sent_h, held_a, other_a, vec, sums, usums),
        None,
        (pieces(wide_j), pieces(wide_j), shape((tokens, D), F32)),
        None,
        22,
        scratch=[pltpu.VMEM((D, 3 * D), BF16)],
    )
    parts_j = links.exchange(kept_j, sent_j)
    parts_d = links.reduce(parts_d, hops["d"][2])
    parts_i = links.reduce(parts_i, hops["i"][1])
    parts_j = links.reduce(parts_j, hops["j"][0])
    block_out = call(
        "down",
        functools.partial(down_kernel, slots_c, ff_rows),
        (place, slot_mask, active, middle, held_c, other_c, vec),
        [SMEM, SMEM, tiled(size, same), fixed(size, D), block_c, block_c, fixed(16, D)],
        shape((tokens, D), BF16),
        fixed(tokens, D),
        18,
        grid=(depth,),
        scratch=[pltpu.VMEM((D, D), BF16), pltpu.VMEM((size, D), F32)],
    )
    parts_i = links.reduce(parts_i, hops["i"][2])
    parts_j = links.reduce(parts_j, hops["j"][1])
    parts_u = links.reduce(parts_u, hops["u"][2])
    parts_j = links.reduce(parts_j, hops["j"][2])
    parts_u = links.reduce(parts_u, hops["u"][3])
    parts_i = links.reduce(parts_i, hops["i"][3])
    parts_d = links.reduce(parts_d, hops["d"][3])
    parts_j = links.reduce(parts_j, hops["j"][3])
    grads_d, grads_u, grads_i, grads_j = (settle(parts) for parts in (parts_d, parts_u, parts_i, parts_j))
    half = D // 2
    grads_packed = []
    for part in range(3):
        grads_packed += [grads_i[:, D + part * half : D + (part + 1) * half], grads_j[:, part * half : (part + 1) * half]]
    small = grads_j[:, 3 * half : 3 * half + 8 + wide].T
    return (
        block_out,
        igrad,
        small[0],
        small[1],
        jnp.concatenate(grads_packed, axis=1),
        small[2],
        small[3],
        grads_i[:, :D],
        small[4],
        small[5],
        small[6],
        grads_u,
        small[8:].reshape(-1),
        grads_d,
        small[7],
    )


def solution(mesh):
    row, flat = P("dp", None), P("dp")
    in_specs = (row, flat, flat, flat, row, flat, flat, row, flat, flat, flat, row, flat, row, flat, row)
    out_specs = (row, row, flat, flat, row, flat, flat, row, flat, flat, flat, row, flat, row, flat)
    return jax.shard_map(shards, mesh=mesh, in_specs=in_specs, out_specs=out_specs, check_vma=False)
```

```python
import functools

import jax
import jax.numpy as jnp
from jax import lax
from jax.experimental import pallas as pl
from jax.experimental.pallas import tpu as pltpu
from jax.sharding import PartitionSpec as P

D = 768
HEADS = 12
HEAD_DIM = 64
FF = 3072
LEN = 197
SLOT = 208
SPEED = 1.15e9
LENGTHS = (1, 8, 1, 0.5, 24, 1, 1, 24, 0.25, 1, 2, 0.25, 1, 8, 3, 24, 1, 0.25, 0.25, 8, 2, 6, 12, 32, 1, 2, 1, 16, 2, 1, 32, 2, 1, 32, 4, 0.5, 2, 0.5, 6, 8, 0.5, 2, 24, 12)
ORDERS = {'a': 'fnxx', 'b': 'fxnx', 'e': 'xfxn', 'c': 'nxfx', 'd': 'xnfx', 'u': 'xnxf', 'i': 'xxfn', 'j': 'xxnf'}
GATHERS = ("a", "b", "e", "c")
FIRST = 2
PINNED = {}
SCALE = HEAD_DIM ** (-0.5)
F32 = jnp.float32
BF16 = jnp.bfloat16
VMEM = pl.BlockSpec(memory_space=pltpu.VMEM)
SMEM = pl.BlockSpec(memory_space=pltpu.SMEM)
ANY = pl.BlockSpec(memory_space=pl.ANY)
TOKEN = pltpu.HBM((8, 128), F32)


def params(megabytes):
    return pltpu.CompilerParams(
        vmem_limit_bytes=megabytes << 20, dimension_semantics=("arbitrary",)
    )


def cost(length):
    return pl.CostEstimate(flops=int(length * SPEED), transcendentals=0, bytes_accessed=D)


def mul(a, b):
    return jnp.dot(a, b, preferred_element_type=F32)


def mul_t(a, b):
    return lax.dot_general(a, b, (((1,), (1,)), ((), ())), preferred_element_type=F32)


def t_mul(a, b):
    return lax.dot_general(a, b, (((0,), (0,)), ((), ())), preferred_element_type=F32)


class Links:
    def __init__(self, count):
        chips = count // 2
        z = min(4, chips)
        plane = chips // z
        x = 1
        while x * x < plane:
            x *= 2
        self.count, self.z, self.plane = count, z, plane
        bit = 2
        x_bits, y_bits, z_bits = [], [], []
        for bits, extent in ((x_bits, x), (y_bits, plane // x), (z_bits, z)):
            size = 1
            while size < extent:
                bits.append(bit)
                bit *= 2
                size *= 2
        across = list(zip(x_bits + y_bits, y_bits + x_bits))
        half = (len(across) + 1) // 2
        self.near = [(b, b) for b in z_bits[:1]]
        self.far = [(b, b) for b in z_bits[1:]]
        self.across = across[:half], across[half:]
        self.all = self.near + self.far + across
        index = lax.axis_index("dp")
        core = index % 2
        sides = [((index & jnp.where(core == 0, *step)) != 0).astype(jnp.int32) for step in self.all]
        self.place = jnp.stack([core.astype(jnp.int32)] + sides)
        self.last = None
        self.lengths = iter(LENGTHS + (1,) * 64)

    def length(self):
        return next(self.lengths)

    def hops(self, order):
        found, crossed = [], 0
        for kind in order:
            if kind == "x":
                found.append(self.across[crossed])
                crossed += 1
            else:
                found.append(self.far if kind == "f" else self.near)
        return found

    def steps(self, order, scatter):
        steps = [step for hop in self.hops(order) for step in hop]
        return steps[::-1] if scatter else steps

    def slots(self, order, scatter):
        steps = self.steps(order, scatter)
        found = []
        for device in range(self.count):
            bits = [1 if device & step[device % 2] else 0 for step in steps]
            found.append((device % 2, sum(b << weight for weight, b in enumerate(bits))))
        return tuple(found)

    def tiles(self, order, scatter):
        steps = self.steps(order, scatter)[::-1]
        along = [step in self.near or step in self.far for step in steps]
        block = tuple(1 if z else 2 for z in along)

        def index(t):
            return tuple((t % 2 if step in self.near else t // 2) if z else 0 for step, z in zip(steps, along))

        found = []
        for device in range(self.count // self.z):
            found.append((device % 2, tuple(1 if device & step[device % 2] else 0 for step in steps)))
        return (2,) * len(steps), block, index, tuple(found)

    def run(self, kernel, *args, **options):
        *out, self.last = kernel(self.last, *args, **options)
        return tuple(out)

    def swap(self, value, even, odd):
        pairs = [(i, i ^ (odd if i % 2 else even)) for i in range(self.count)]
        return lax.ppermute(value, "dp", pairs)

    def pair(self, step, held, other):
        count, rows, width = held.shape
        at = self.all.index(step)

        def body(place, held, other, *refs):
            out = refs[-2]
            high = place[1 + at]

            def copy(i, carry):
                out[high, i] = held[i]
                out[1 - high, i] = other[i]
                return carry

            lax.fori_loop(0, count, copy, 0)

        def kernel(last):
            return pl.pallas_call(
                body,
                out_shape=(jax.ShapeDtypeStruct((2, count, rows, width), BF16), TOKEN),
                in_specs=[SMEM, VMEM, VMEM] + ([] if last is None else [ANY]),
                out_specs=(VMEM, ANY),
                compiler_params=pltpu.CompilerParams(vmem_limit_bytes=10 << 20),
                cost_estimate=cost(self.length()),
                name="pair",
            )(self.place, held, other, *([] if last is None else [pinned(last)]))

        return self.run(kernel)[0].reshape(2 * count, rows, width)

    def advance(self, held, hop):
        for step in hop:
            held = self.pair(step, held, self.swap(held, *step))
        return held

    def exchange(self, kept, sent):
        other = self.swap(sent, 1, 1)
        shape = (-1,) + kept.shape[-2:]
        return kept.reshape(shape), other.reshape(shape)

    def halve(self, step, kept, other):
        at = self.all.index(step)
        half = kept.shape[0] // 2
        chunk = max(1, half // 4)
        grid = half // chunk
        block = (chunk,) + kept.shape[1:]
        upper = pl.BlockSpec(block, lambda i, place: (place[1 + at] * grid + i, 0, 0))
        lower = pl.BlockSpec(block, lambda i, place: ((1 - place[1 + at]) * grid + i, 0, 0))
        straight = pl.BlockSpec(block, lambda i, place: (i, 0, 0))

        def body(place, kept_up, kept_low, other_up, other_low, last, stay, leave, token):
            stay[...] = kept_up[...].astype(F32) + other_up[...].astype(F32)
            leave[...] = (kept_low[...].astype(F32) + other_low[...].astype(F32)).astype(BF16)

        def kernel(last):
            return pl.pallas_call(
                body,
                grid_spec=pltpu.PrefetchScalarGridSpec(
                    num_scalar_prefetch=1,
                    grid=(grid,),
                    in_specs=[upper, lower, upper, lower, ANY],
                    out_specs=(straight, straight, ANY),
                ),
                out_shape=(
                    jax.ShapeDtypeStruct((half,) + kept.shape[1:], F32),
                    jax.ShapeDtypeStruct((half,) + kept.shape[1:], BF16),
                    TOKEN,
                ),
                compiler_params=params(12),
                cost_estimate=cost(self.length()),
                name="halve",
            )(self.place, kept, kept, other, other, pinned(last))

        return self.run(kernel)

    def reduce(self, parts, hop):
        for step in hop:
            kept, low = self.halve(step, *parts)
            parts = kept, self.swap(low, *step)
        return parts


def pinned(value):
    return pltpu.with_memory_space_constraint(value, pltpu.HBM)


def settle(parts):
    return parts[0][0].astype(F32) + parts[1][0].astype(F32)


def collect(into, rows, slots, core, held, other, cols=slice(None)):
    @pl.when(core == 0)
    def _():
        for place, (parity, piece) in enumerate(slots):
            source = other if parity else held
            into[place * rows : (place + 1) * rows, :] = source[piece + (slice(None), cols)]

    @pl.when(core == 1)
    def _():
        for place, (parity, piece) in enumerate(slots):
            source = held if parity else other
            into[place * rows : (place + 1) * rows, :] = source[piece + (slice(None), cols)]


def deal(values, rows, slots, core, kept, sent, cols=slice(None)):
    halves = ({}, {})
    for place, (parity, piece) in enumerate(slots):
        halves[parity][piece] = values[place * rows : (place + 1) * rows, :]
    for piece, even in halves[0].items():
        odd = halves[1][piece]
        kept[piece + (slice(None), cols)] = jnp.where(core == 0, even, odd)
        sent[piece + (slice(None), cols)] = jnp.where(core == 0, odd, even)


def standard(values):
    centred = values - jnp.mean(values, axis=-1, keepdims=True)
    rate = lax.rsqrt(jnp.mean(centred * centred, axis=-1, keepdims=True) + 1e-06)
    return centred * rate, rate


def standard_back(grad, gain, standardised, rate):
    pushed = grad * gain
    along = jnp.mean(pushed * standardised, axis=-1, keepdims=True)
    inner = pushed - jnp.mean(pushed, axis=-1, keepdims=True) - standardised * along
    sums = (jnp.sum(grad * standardised, axis=0, keepdims=True), jnp.sum(grad, axis=0, keepdims=True))
    return (rate * inner,) + sums


def first_half(width):
    return lax.broadcasted_iota(jnp.int32, (SLOT, 2 * HEAD_DIM), 1) < HEAD_DIM


def line_up_kernel(weight, *refs):
    lines, bias, out = refs[:8], refs[8], refs[-1]
    rows = weight.shape[0]
    out[0, :, : 3 * D] = weight[...]
    lines = [line[...].astype(F32).reshape(1, rows) for line in lines]
    bias = bias[...].astype(F32).reshape(1, -1)
    lines += [bias[:, at : at + rows] for at in range(0, bias.shape[1], rows)]
    lines.append(jnp.zeros((128 - len(lines), rows), F32))
    out[0, :, 3 * D :] = jnp.concatenate(lines, axis=0).T.astype(BF16)


def spread_kernel(images, live, block_in, cotangent, earlier, x_ref, dm_ref):
    for ref, into in ((block_in, x_ref), (cotangent, dm_ref)):
        values = ref[...].astype(F32)
        for image in range(images):
            part = values[image * LEN : (image + 1) * LEN]
            if into is dm_ref:
                part = jnp.where(live[image * LEN] != 0, part, 0.0)
            part = jnp.concatenate([part, jnp.zeros((SLOT - LEN, D), F32)], axis=0)
            into[image * SLOT : (image + 1) * SLOT, :] = part.astype(BF16)


def trim(values):
    parts = [values[at : at + LEN] for at in range(0, values.shape[0], SLOT)]
    return jnp.concatenate(parts, axis=0)


def join_kernel(ranges, *refs):
    out = refs[-1]
    start = 0
    for part, (first, last) in zip(refs, ranges):
        out[0, :, start : start + last - first] = part[:, first:last]
        start += last - first


def attend_kernel(slots, rows, place, x_ref, held, other, earlier, normed, qkv, attended, lse, vec, weight, columns):
    core = place[0]
    collect(weight, rows, slots, core, held, other, slice(0, 3 * D))
    collect(columns, rows, slots, core, held, other, slice(3 * D, 3 * D + 128))
    vec[...] = columns[...].astype(F32).T[: vec.shape[0], :]
    shaped, _ = standard(x_ref[...].astype(F32))
    low = (shaped * vec[0:1, :] + vec[1:2, :]).astype(BF16)
    normed[...] = low
    for part, row in ((0, 2), (1, None), (2, 3)):
        cols = pl.ds(part * D, D)
        packed = mul(low, weight[:, cols])
        if row is not None:
            packed = packed + vec[row : row + 1, :]
        qkv[:, cols] = packed.astype(BF16)
    left = first_half(0)
    real = lax.broadcasted_iota(jnp.int32, (SLOT, SLOT), 1) < LEN
    lane = lax.broadcasted_iota(jnp.int32, (SLOT, 128), 1)
    images = x_ref.shape[0] // SLOT
    lse[...] = jnp.zeros_like(lse)

    def pair_step(at, carry):
        image, pair = at // (HEADS // 2), at % (HEADS // 2)
        tokens = pl.ds(pl.multiple_of(image * SLOT, 16), SLOT)
        cols = lambda part: pl.ds(pl.multiple_of(part * D + pair * 128, 128), 128)
        query, key, value = qkv[tokens, cols(0)], qkv[tokens, cols(1)], qkv[tokens, cols(2)]
        mixed, logs = [], lse[tokens, :]
        for side in range(2):
            chosen = left if side == 0 else ~left
            scores = mul_t(jnp.where(chosen, query, jnp.zeros_like(query)), key) * SCALE
            scores = jnp.where(real, scores, -1e30)
            top = jnp.max(scores, axis=-1, keepdims=True)
            raised = jnp.exp(scores - top)
            total = jnp.sum(raised, axis=-1, keepdims=True)
            logs = jnp.where(lane == pair * 2 + side, top + jnp.log(total), logs)
            mixed.append(mul((raised * (1.0 / total)).astype(BF16), value))
        lse[tokens, :] = logs
        attended[tokens, cols(0)] = jnp.where(left, mixed[0], mixed[1]).astype(BF16)
        return carry

    lax.fori_loop(0, images * (HEADS // 2), pair_step, 0, unroll=HEADS // 2)


def up_kernel(slots_b, slots_e, slots_d, rows, ff_rows, place, x_ref, attended, dm, held, other, held_e, other_e, vec, ubias, earlier, middle, normed, active, slope, kept, sent, weight):
    core = place[0]
    step = pl.program_id(0)

    @pl.when(step <= FIRST)
    def _():
        collect(weight, rows, slots_b, core, held, other)

    @pl.when(step > FIRST)
    def _():
        collect(weight, rows, slots_e, core, held_e, other_e)

    @pl.when(step == 0)
    def _():
        total = x_ref[...].astype(F32) + mul(attended[...], weight[...]) + vec[4:5, :]
        middle[...] = total
        shaped, _ = standard(total)
        normed[...] = (shaped * vec[5:6, :] + vec[6:7, :]).astype(BF16)

    @pl.when(step > 0)
    def _():
        pre = mul(normed[...], weight[...]) + ubias[0:1, :]
        share = 0.5 + 0.5 * lax.erf(pre * (0.5**0.5))
        low = (pre * share).astype(BF16)
        active[...] = low
        slope[...] = share + pre * (jnp.exp(pre * pre * -0.5) * 0.3989422804014327)
        grad = t_mul(low, dm[...]).astype(BF16)

        deal(grad, ff_rows, slots_d, core, kept, sent)


def slope_kernel(slots_u, slots_c, rows, ff_rows, place, dm, normed, slope, held, other, earlier, low, kept, sent, sums, weight):
    core = place[0]
    collect(weight, ff_rows, slots_c, core, held, other)
    grad = (mul_t(dm[...], weight[...]) * slope[...]).astype(BF16)
    low[...] = grad
    deal(t_mul(normed[...], grad).astype(BF16), rows, slots_u, core, kept, sent)
    lines = jnp.broadcast_to(jnp.sum(grad.astype(F32), axis=0, keepdims=True), (128, grad.shape[1])).T
    lane = lax.broadcasted_iota(jnp.int32, (rows, 128), 1)
    for device in range(grad.shape[1] // ff_rows):
        total = jnp.zeros((rows, 128), F32)
        for at in range(ff_rows // rows):
            start = device * ff_rows + at * rows
            total = jnp.where(lane == 8 + at, lines[start : start + rows, :], total)
        sums[device * rows : (device + 1) * rows, :] = total


def middle_kernel(slots_b, slots_e, slots_i, rows, place, low, middle, dm, attended, held, other, held_e, other_e, vec, earlier, datt, dmid, kept, sent, sums, weight, back):
    core = place[0]
    step = pl.program_id(0)
    last = pl.num_programs(0) - 1

    @pl.when((step < FIRST) | (step == last))
    def _():
        collect(weight, rows, slots_b, core, held, other)

    @pl.when((step >= FIRST) & (step < last))
    def _():
        collect(weight, rows, slots_e, core, held_e, other_e)

    @pl.when(step == 0)
    def _():
        back[...] = mul_t(low[...], weight[...])

    @pl.when((step > 0) & (step < last))
    def _():
        back[...] += mul_t(low[...], weight[...])

    @pl.when(step == last)
    def _():
        source = dm[...].astype(F32)
        shaped, rate = standard(middle[...])
        inner, ggain, gshift = standard_back(back[...], vec[5:6, :], shaped, rate)
        total = source + inner
        dmid[...] = total
        branch = total.astype(BF16)
        datt[...] = mul_t(branch, weight[...]).astype(BF16)
        deal(t_mul(attended[...], branch).astype(BF16), rows, slots_i, core, kept, sent)
        gout = jnp.sum(branch.astype(F32), axis=0, keepdims=True)
        gdown = jnp.sum(source, axis=0, keepdims=True)
        sums[...] = jnp.concatenate([gout, ggain, gshift, gdown] * 2, axis=0)


def down_kernel(slots_c, ff_rows, place, live, active, middle, held, other, vec, earlier, result, weight, mixed):
    core = place[0]
    step = pl.program_id(0)
    collect(weight, ff_rows, slots_c, core, held, other)
    more = mul(active[...], weight[...])

    @pl.when(step == 0)
    def _():
        mixed[...] = more

    @pl.when(step > 0)
    def _():
        mixed[...] += more

    @pl.when(step == pl.num_programs(0) - 1)
    def _():
        full = middle[...] + mixed[...] + vec[7:8, :]
        images = full.shape[0] // SLOT
        keep = [jnp.where(live[i * LEN] != 0, full[i * SLOT : i * SLOT + LEN], 0.0) for i in range(images)]
        result[...] = jnp.concatenate(keep, axis=0).astype(BF16)


def heads_kernel(slots, rows, first, beside, place, qkv, datt, lse, normed, *refs):
    more, (earlier, dqkv, kept, sent) = refs[:-4], refs[-4:]
    core = place[0]
    left = first_half(0)
    real = lax.broadcasted_iota(jnp.int32, (SLOT, SLOT), 1) < LEN
    lane = lax.broadcasted_iota(jnp.int32, (SLOT, 128), 1)
    pairs = HEADS // 4
    images = qkv.shape[0] // SLOT
    for source, into in zip(more, (kept, sent)):
        into[:, :, :beside] = source[...]

    def pair_step(at, carry):
        image, local = at // pairs, at % pairs
        pair = first + local
        tokens = pl.ds(pl.multiple_of(image * SLOT, 16), SLOT)
        cols = lambda part: pl.ds(pl.multiple_of(part * D + pair * 128, 128), 128)
        query, key, value = qkv[tokens, cols(0)], qkv[tokens, cols(1)], qkv[tokens, cols(2)]
        grad, logs = datt[tokens, cols(0)], lse[tokens, :]
        dq, dk, dv = [], [], []
        for side in range(2):
            chosen = left if side == 0 else ~left
            scores = mul_t(jnp.where(chosen, query, jnp.zeros_like(query)), key) * SCALE
            log = jnp.sum(jnp.where(lane == pair * 2 + side, logs, 0.0), axis=-1, keepdims=True)
            attn = jnp.where(real, jnp.exp(scores - log), 0.0)
            dattn = mul_t(jnp.where(chosen, grad, jnp.zeros_like(grad)), value)
            dscores = (attn * (dattn - jnp.sum(attn * dattn, axis=-1, keepdims=True))).astype(BF16)
            dv.append(t_mul(attn.astype(BF16), grad))
            dq.append(mul(dscores, key) * SCALE)
            dk.append(t_mul(dscores, query) * SCALE)
        for part, halves in ((0, dq), (1, dk), (2, dv)):
            into = pl.ds(pl.multiple_of(part * (D // 2) + local * 128, 128), 128)
            dqkv[tokens, into] = jnp.where(left, halves[0], halves[1]).astype(BF16)
        return carry

    lax.fori_loop(0, images * pairs, pair_step, 0, unroll=images * pairs)
    grad = t_mul(normed[...], dqkv[...]).astype(BF16)
    deal(grad, rows, slots, core, kept, sent, slice(beside, beside + 3 * D // 2))


def input_kernel(slots_a, slots_j, rows, place, x_ref, dmid, half_a, half_b, kept_b, sent_b, held, other, vec, sums, usums, earlier, kept, sent, igrad, weight):
    core = place[0]
    for source, into in ((kept_b, kept), (sent_b, sent)):
        into[:, :, : source.shape[2]] = source[...]
    collect(weight, rows, slots_a, core, held, other, slice(0, 3 * D))
    back = None
    rowsums = []
    for part in range(3):
        cols = pl.ds(part * (D // 2), D // 2)
        low = jnp.concatenate([half_a[:, cols], half_b[:, cols]], axis=1)
        rowsums.append(jnp.sum(low.astype(F32), axis=0, keepdims=True))
        more = mul_t(low, weight[:, pl.ds(part * D, D)])
        back = more if back is None else back + more
    shaped, rate = standard(x_ref[...].astype(F32))
    inner, ggain, gshift = standard_back(back, vec[0:1, :], shaped, rate)
    igrad[...] = trim(dmid[...] + inner)
    lines = [ggain, gshift, rowsums[0], rowsums[2], sums[0:4, :]]
    lines.append(jnp.zeros((128 - 8, D), F32))
    columns = (jnp.concatenate(lines, axis=0).T + usums[...]).astype(BF16)
    deal(columns, rows, slots_j, core, kept, sent, slice(kept_b.shape[2], kept_b.shape[2] + 128))


def zeroed(piece, part):
    return tuple(0 if extent == 1 else bit for bit, extent in zip(piece, part))


def shards(
    block_in,
    slot_mask,
    gain_first,
    shift_first,
    packed_weight,
    query_bias,
    value_bias,
    out_weight,
    out_bias,
    gain_second,
    shift_second,
    up_weight,
    up_bias,
    down_weight,
    down_bias,
    cotangent,
):
    links = Links(lax.axis_size("dp"))
    rows = packed_weight.shape[0]
    ff_rows = down_weight.shape[0]
    wide = ff_rows // rows
    count, depth = links.count, links.z
    number = count // 2
    place = links.place
    tokens = block_in.shape[0]
    images = tokens // LEN
    size = images * SLOT
    hops = {group: links.hops(order) for group, order in ORDERS.items()}
    slots = {group: links.slots(order, group not in GATHERS) for group, order in ORDERS.items()}
    flat = {group: tuple((parity, (piece,)) for parity, piece in found) for group, found in slots.items()}
    shape = jax.ShapeDtypeStruct
    pieces = lambda cols: shape((number, rows, cols), BF16)
    fixed = lambda height, width: pl.BlockSpec((height, width), lambda t: (0, 0))
    tile = FF // depth
    tiled = lambda height, at: pl.BlockSpec((height, tile), lambda t: (0, at(t)))
    whole = lambda cols: pl.BlockSpec((number, rows, cols), lambda t: (0, 0, 0))
    before = lambda t: jnp.maximum(t - 1, 0)
    upto = lambda t: jnp.minimum(t, depth - 1)
    same = lambda t: t
    view_c, part_c, at_c, slots_c = links.tiles(ORDERS["c"], False)
    view_d, part_d, at_d, slots_d = links.tiles(ORDERS["d"], True)
    slots_c, slots_d = (tuple((parity, zeroed(piece, part)) for parity, piece in found) for found, part in ((slots_c, part_c), (slots_d, part_d)))
    zeros = (0, 0)
    block_c = pl.BlockSpec(part_c + (ff_rows, D), lambda t: at_c(t) + zeros)

    def call(name, kernel, ins, specs, outs, out_specs, megabytes, grid=None, scratch=()):
        many = isinstance(outs, tuple)
        if specs is None:
            specs = [SMEM if v is place or v is slot_mask else VMEM for v in ins]
            out_specs = (VMEM,) * (len(outs) if many else 1)
        elif not many:
            out_specs = (out_specs,)
        outs = outs if many else (outs,)
        body = kernel
        token = len(ins) + (links.last is not None) + len(outs)

        def kernel(*refs):
            return body(*refs[:token], *refs[token + 1 :])

        far = {(size, FF)} if name not in PINNED else {(size, FF)} | PINNED[name](size)
        outs = tuple(pltpu.HBM(o.shape, o.dtype) if o.shape in far else o for o in outs)
        streamed = lambda v: v.shape in far or (v.ndim > 2 and name in ("up", "slope", "middle", "down"))
        ins = tuple(pinned(v) if streamed(v) else v for v in ins)
        if grid is not None:
            compiler = params(megabytes)
        else:
            compiler = pltpu.CompilerParams(vmem_limit_bytes=megabytes << 20)

        def launch(last):
            return pl.pallas_call(
                kernel,
                out_shape=outs + (TOKEN,),
                in_specs=list(specs) + ([] if last is None else [ANY]),
                out_specs=tuple(out_specs) + (ANY,),
                scratch_shapes=list(scratch),
                compiler_params=compiler,
                cost_estimate=cost(links.length()),
                name=name,
                **({} if grid is None else {"grid": grid}),
            )(*ins, *([] if last is None else [pinned(last)]))

        out = links.run(launch)
        return out if many else out[0]

    def joined(*parts):
        arrays = tuple(part[0] for part in parts)
        ranges = tuple((first, last) for _, first, last in parts)
        width = sum(last - first for first, last in ranges)
        out = shape((1, arrays[0].shape[0], width), BF16)
        return call("join", functools.partial(join_kernel, ranges), arrays, None, out, None, 8)

    split = FIRST * tile
    vectors = (gain_first, shift_first, query_bias, value_bias, out_bias, gain_second, shift_second, down_bias, up_bias)
    wide_a = 3 * D + 128
    gather_a = call("line_up", line_up_kernel, (packed_weight,) + vectors, None, shape((1, rows, wide_a), BF16), None, 60)
    gather_e = joined((up_weight, split, FF))
    gather_b = joined((out_weight, 0, D), (up_weight, 0, split))
    gather_a = links.advance(gather_a, hops["a"][0])
    gather_c = down_weight[None]
    gather_c = links.advance(gather_c, hops["c"][0])
    gather_b = links.advance(gather_b, hops["b"][0])
    gather_e = links.advance(gather_e, hops["e"][0])
    gather_a = links.advance(gather_a, hops["a"][1])
    gather_b = links.advance(gather_b, hops["b"][1])
    x, dm = call(
        "spread",
        functools.partial(spread_kernel, images),
        (slot_mask, block_in, cotangent),
        None,
        (shape((size, D), BF16), shape((size, D), BF16)),
        None,
        16,
    )
    gather_c = links.advance(gather_c, hops["c"][1])
    gather_a = links.advance(gather_a, hops["a"][2])
    gather_e = links.advance(gather_e, hops["e"][1])
    gather_b = links.advance(gather_b, hops["b"][2])
    gather_a = links.advance(gather_a, hops["a"][3])
    held_a, other_a = gather_a, links.swap(gather_a, 1, 1)
    gather_e = links.advance(gather_e, hops["e"][2])
    gather_c = links.advance(gather_c, hops["c"][2])
    normed, qkv, attended, lse, vec = call(
        "attend",
        functools.partial(attend_kernel, flat["a"], rows),
        (place, x, held_a, other_a),
        None,
        (
            shape((size, D), BF16),
            shape((size, 3 * D), BF16),
            shape((size, D), BF16),
            shape((size, 128), F32),
            shape((16, D), F32),
        ),
        None,
        20,
        scratch=[pltpu.VMEM((D, 3 * D), BF16), pltpu.VMEM((D, 128), BF16)],
    )
    ubias = vec[8 : 8 + wide].reshape(wide, count, rows).transpose(1, 0, 2).reshape(1, FF)
    gather_b = links.advance(gather_b, hops["b"][3])
    held_b, other_b = gather_b, links.swap(gather_b, 1, 1)
    gather_e = links.advance(gather_e, hops["e"][3])
    held_e, other_e = gather_e, links.swap(gather_e, 1, 1)
    gather_c = links.advance(gather_c, hops["c"][3])
    held_c, other_c = gather_c.reshape(view_c + (ff_rows, D)), links.swap(gather_c, 1, 1).reshape(view_c + (ff_rows, D))
    block_b = pl.BlockSpec((number, rows, D), lambda t: (0, 0, jnp.minimum(t, FIRST)))
    block_e = pl.BlockSpec((number, rows, D), lambda t: (0, 0, jnp.maximum(t - FIRST - 1, 0)))
    dealt = pl.BlockSpec(part_d + (ff_rows, D), lambda t: at_d(before(t)) + zeros)
    middle, normed_two, active, slope, kept_d, sent_d = call(
        "up",
        functools.partial(up_kernel, flat["b"], flat["e"], slots_d, rows, ff_rows),
        (place, x, attended, dm, held_b, other_b, held_e, other_e, vec, ubias),
        [SMEM] + [fixed(size, D)] * 3 + [block_b, block_b, block_e, block_e, fixed(16, D), tiled(1, before)],
        (
            shape((size, D), F32),
            shape((size, D), BF16),
            shape((size, FF), BF16),
            shape((size, FF), F32),
            shape(view_d + (ff_rows, D), BF16),
            shape(view_d + (ff_rows, D), BF16),
        ),
        (fixed(size, D), fixed(size, D), tiled(size, before), tiled(size, before), dealt, dealt),
        30,
        grid=(depth + 1,),
        scratch=[pltpu.VMEM((D, D), BF16)],
    )
    parts_d = links.exchange(kept_d, sent_d)
    block_u = pl.BlockSpec((number, rows, D), lambda t: (0, 0, t))
    low, kept_u, sent_u, usums = call(
        "slope",
        functools.partial(slope_kernel, flat["u"], slots_c, rows, ff_rows),
        (place, dm, normed_two, slope, held_c, other_c),
        [SMEM, fixed(size, D), fixed(size, D), tiled(size, same), block_c, block_c],
        (shape((size, FF), BF16), pieces(FF), pieces(FF), shape((D, 128), F32)),
        (tiled(size, same), block_u, block_u, pl.BlockSpec((D // depth, 128), lambda t: (t, 0))),
        22,
        grid=(depth,),
        scratch=[pltpu.VMEM((D, D), BF16)],
    )
    parts_u = links.exchange(kept_u, sent_u)
    parts_d = links.reduce(parts_d, hops["d"][0])
    block_b = pl.BlockSpec((number, rows, D), lambda t: (0, 0, jnp.where(t == depth, 0, jnp.minimum(t + 1, FIRST))))
    block_e = pl.BlockSpec((number, rows, D), lambda t: (0, 0, jnp.clip(t - FIRST, 0, depth - FIRST - 1)))
    datt, dmid, kept_o, sent_o, sums = call(
        "middle",
        functools.partial(middle_kernel, flat["b"], flat["e"], flat["i"], rows),
        (place, low, middle, dm, attended, held_b, other_b, held_e, other_e, vec),
        [SMEM, tiled(size, upto)] + [fixed(size, D)] * 3 + [block_b, block_b, block_e, block_e, fixed(16, D)],
        (shape((size, D), BF16), shape((size, D), F32), pieces(D), pieces(D), shape((8, D), F32)),
        (fixed(size, D), fixed(size, D), whole(D), whole(D), fixed(8, D)),
        26,
        grid=(depth + 1,),
        scratch=[pltpu.VMEM((D, D), BF16), pltpu.VMEM((size, D), F32)],
    )
    parts_u = links.reduce(parts_u, hops["u"][0])
    def heads(group, first, beside, *more):
        cols = beside + 3 * D // 2
        return call(
            "heads",
            functools.partial(heads_kernel, flat[group], rows, first, beside),
            (place, qkv, datt, lse, normed) + more,
            None,
            (shape((size, 3 * D // 2), BF16), pieces(cols), pieces(cols)),
            None,
            16,
        )

    half_a, kept_i, sent_i = heads("i", 0, D, kept_o, sent_o)
    parts_i = links.exchange(kept_i, sent_i)
    parts_d = links.reduce(parts_d, hops["d"][1])
    half_b, kept_h, sent_h = heads("j", HEADS // 4, 0)
    parts_i = links.reduce(parts_i, hops["i"][0])
    parts_u = links.reduce(parts_u, hops["u"][1])
    wide_j = 3 * D // 2 + 128
    kept_j, sent_j, igrad = call(
        "inward",
        functools.partial(input_kernel, flat["a"], flat["j"], rows),
        (place, x, dmid, half_a, half_b, kept_h, sent_h, held_a, other_a, vec, sums, usums),
        None,
        (pieces(wide_j), pieces(wide_j), shape((tokens, D), F32)),
        None,
        22,
        scratch=[pltpu.VMEM((D, 3 * D), BF16)],
    )
    parts_j = links.exchange(kept_j, sent_j)
    parts_d = links.reduce(parts_d, hops["d"][2])
    parts_i = links.reduce(parts_i, hops["i"][1])
    parts_j = links.reduce(parts_j, hops["j"][0])
    block_out = call(
        "down",
        functools.partial(down_kernel, slots_c, ff_rows),
        (place, slot_mask, active, middle, held_c, other_c, vec),
        [SMEM, SMEM, tiled(size, same), fixed(size, D), block_c, block_c, fixed(16, D)],
        shape((tokens, D), BF16),
        fixed(tokens, D),
        18,
        grid=(depth,),
        scratch=[pltpu.VMEM((D, D), BF16), pltpu.VMEM((size, D), F32)],
    )
    parts_i = links.reduce(parts_i, hops["i"][2])
    parts_j = links.reduce(parts_j, hops["j"][1])
    parts_u = links.reduce(parts_u, hops["u"][2])
    parts_j = links.reduce(parts_j, hops["j"][2])
    parts_u = links.reduce(parts_u, hops["u"][3])
    parts_i = links.reduce(parts_i, hops["i"][3])
    parts_d = links.reduce(parts_d, hops["d"][3])
    parts_j = links.reduce(parts_j, hops["j"][3])
    grads_d, grads_u, grads_i, grads_j = (settle(parts) for parts in (parts_d, parts_u, parts_i, parts_j))
    half = D // 2
    grads_packed = []
    for part in range(3):
        grads_packed += [grads_i[:, D + part * half : D + (part + 1) * half], grads_j[:, part * half : (part + 1) * half]]
    small = grads_j[:, 3 * half : 3 * half + 8 + wide].T
    return (
        block_out,
        igrad,
        small[0],
        small[1],
        jnp.concatenate(grads_packed, axis=1),
        small[2],
        small[3],
        grads_i[:, :D],
        small[4],
        small[5],
        small[6],
        grads_u,
        small[8:].reshape(-1),
        grads_d,
        small[7],
    )


def solution(mesh):
    row, flat = P("dp", None), P("dp")
    in_specs = (row, flat, flat, flat, row, flat, flat, row, flat, flat, flat, row, flat, row, flat, row)
    out_specs = (row, row, flat, flat, row, flat, flat, row, flat, flat, flat, row, flat, row, flat)
    return jax.shard_map(shards, mesh=mesh, in_specs=in_specs, out_specs=out_specs, check_vma=False)
```
